32 devices in a mesh: orbit: 8 (over y, x, core), tile: 4 (over z).
Axes of the slice: x: 2, y: 2, z: 4, core: 2. Of those that a mesh axis runs over, the one named last changes fastest.
Arguments:
- tokens: bfloat16 [32, 256, 1280], P('orbit', 'tile'), may hold values from -6 to 6
- cotangent: bfloat16 [32, 256, 1280], P('orbit', 'tile'), may hold values from -60 to 60
- w_query: bfloat16 [1280, 1280], replicated, may hold values from -0.15625 to 0.15625
- w_key: bfloat16 [1280, 1280], replicated, may hold values from -0.15625 to 0.15625
- w_value: bfloat16 [1280, 1280], replicated, may hold values from -0.15625 to 0.15625
- conv_taps: float32 [3, 1280], replicated, may hold values from 0.3 to 1
- conv_bias: float32 [1280], replicated, may hold values from -2 to 2
Outputs:
- grad_tokens: bfloat16 [32, 256, 1280], P('orbit', 'tile')
The draws below stay inside these ranges and needn't reach their ends.
All inputs are finite; a program needn't handle non-finite values.
Results may differ from the reference program's by a relative error of at most 0.009.
The reference program's roundings to bfloat16 on the way count: a program that leaves them out, or rounds other values in their place, can miss the bound.
Values may be sent and summed in bfloat16 or wider, within the bound.
No kernel may reach another device: no remote copies, remote signals or barrier semaphores. Data moves between devices by JAX's collectives and lax.ppermute only.
A program may use at most 64 MiB of HBM per device.

```python
import math
import jax
import jax.numpy as jnp
from jax import lax

C = 1280
HEAD_DIM = 64
TOK_DEV = 64
FRAMES = 32
SPATIAL = 256
N_TILE = 4


def draw_tokens(key, part):
    keys_split = jax.random.split(key, 1)
    sample = jax.random.normal(keys_split[0], (FRAMES, SPATIAL, C), jnp.float32)
    return jnp.clip(sample, -6.0, 6.0).astype(jnp.bfloat16)


def draw_cotangent(key, part):
    keys_split = jax.random.split(key, 4)
    position = jnp.arange(SPATIAL, dtype=jnp.float32) / SPATIAL
    row_jitter = jax.random.uniform(keys_split[1], (SPATIAL,), jnp.float32, -0.5, 0.5)
    row_level = jnp.exp(math.log(10.0) * position + row_jitter)[None, :, None]
    column_level = 0.3 * jnp.exp(jax.random.uniform(keys_split[2], (C,), jnp.float32, 0.0, math.log(10.0)))[None, None, :]
    frame_level = jnp.exp(jax.random.uniform(keys_split[3], (FRAMES,), jnp.float32, -0.5, 0.5))[:, None, None]
    sample = jnp.clip(jax.random.normal(keys_split[0], (FRAMES, SPATIAL, C), jnp.float32), -3.0, 3.0)
    return jnp.clip(sample * row_level * column_level * frame_level, -60.0, 60.0).astype(jnp.bfloat16)


def bell_draw(stream_key, extent, width, limit, held_as=jnp.bfloat16):
    entries = jax.random.normal(stream_key, extent, jnp.float32) * width
    return jnp.minimum(jnp.maximum(entries, -limit), limit).astype(held_as)


def setup_inputs(seed: int = 0) -> dict:
    streams_of = jax.random.split(jax.random.key(seed), 8)
    return {
        "tokens": draw_tokens(jax.random.fold_in(streams_of[7], 71), 0),
        "cotangent": draw_cotangent(jax.random.fold_in(streams_of[7], 71), 0),
        "w_query": bell_draw(streams_of[2], (C, C), C ** -0.5, 0.15625),
        "w_key": bell_draw(streams_of[3], (C, C), C ** -0.5, 0.15625),
        "w_value": bell_draw(streams_of[4], (C, C), C ** -0.5, 0.15625),
        "conv_taps": jnp.clip(jnp.exp(jax.random.uniform(streams_of[5], (3, C), jnp.float32, math.log(0.3), math.log(1.0))), 0.3, 1.0),
        "conv_bias": bell_draw(streams_of[6], (C,), 0.5, 2.0, jnp.float32),
    }


def round_trip(signal):
    return lax.optimization_barrier(signal.astype(jnp.bfloat16)).astype(jnp.float32)

def temporal_mix(signal, conv_taps):
    return conv_taps[0] * jnp.roll(signal, 1, axis=0) + conv_taps[1] * signal + conv_taps[2] * jnp.roll(signal, -1, axis=0)

def temporal_unmix(signal, conv_taps):
    return signal + conv_taps[0] * jnp.roll(signal, -1, axis=0) + conv_taps[1] * signal + conv_taps[2] * jnp.roll(signal, 1, axis=0)

def attention_grads(query_rows, key_rows, value_rows, grad_rows):
    frames, tok_count, channels = query_rows.shape
    head_count = channels // HEAD_DIM
    inv_root = 1.0 / math.sqrt(HEAD_DIM)
    shape_heads = (frames, tok_count, head_count, HEAD_DIM)
    q_heads = query_rows.astype(jnp.float32).reshape(shape_heads)
    k_heads = key_rows.astype(jnp.float32).reshape(shape_heads)
    v_heads = value_rows.astype(jnp.float32).reshape(shape_heads)
    g_heads = grad_rows.astype(jnp.float32).reshape(shape_heads)
    scores = jnp.einsum('fshd,gshd->shfg', q_heads, k_heads) * inv_root
    peak = lax.optimization_barrier(jnp.max(scores, axis=-1, keepdims=True))
    expo_terms = jnp.exp(scores - peak)
    attn_prob = expo_terms / lax.optimization_barrier(jnp.sum(expo_terms, axis=-1, keepdims=True))
    prob_low = round_trip(attn_prob)
    attn_out = jnp.einsum('shfg,gshd->fshd', prob_low, v_heads)
    row_delta = lax.optimization_barrier(jnp.sum(g_heads * attn_out, axis=-1))
    grad_value = jnp.einsum('shfg,fshd->gshd', prob_low, g_heads).astype(jnp.bfloat16)
    grad_prob = jnp.einsum('fshd,gshd->shfg', g_heads, v_heads)
    d_scores = attn_prob * (grad_prob - jnp.transpose(row_delta, (1, 2, 0))[..., None])
    scores_low = round_trip(d_scores)
    grad_query = (jnp.einsum('shfg,gshd->fshd', scores_low, k_heads) * inv_root).astype(jnp.bfloat16)
    grad_key = (jnp.einsum('shfg,fshd->gshd', scores_low, q_heads) * inv_root).astype(jnp.bfloat16)
    full_shape = (frames, tok_count, channels)
    return (grad_query.reshape(full_shape), grad_key.reshape(full_shape), grad_value.reshape(full_shape))

def attend_block(block):
    return attention_grads(block[0], block[1], block[2], block[3])

def reference(tokens, cotangent, w_query, w_key, w_value, conv_taps, conv_bias):
    frames, spatial, channels = tokens.shape
    source = tokens.astype(jnp.float32)
    hidden = (source + temporal_mix(source, conv_taps) + conv_bias).astype(jnp.bfloat16)
    flat_rows = hidden.reshape(frames * spatial, channels)
    projected = tuple((jnp.dot(flat_rows, weight, preferred_element_type=jnp.float32).astype(jnp.bfloat16).reshape(frames, spatial, channels) for weight in (w_query, w_key, w_value)))
    grad_f = cotangent.astype(jnp.float32)
    energy = lax.optimization_barrier(jnp.sum(grad_f * grad_f, axis=(1, 2)))
    factor = lax.rsqrt(energy / (spatial * channels) + 1e-06)
    grad_out = (grad_f * factor[:, None, None]).astype(jnp.bfloat16)
    stacked = tuple((jnp.moveaxis(member.reshape(frames, N_TILE, TOK_DEV, channels), 1, 0) for member in (projected[0], projected[1], projected[2], grad_out)))
    results = lax.map(attend_block, stacked)
    grads = tuple((jnp.moveaxis(member, 0, 1).reshape(frames * spatial, channels) for member in results))
    grad_hidden = (jnp.dot(grads[0], w_query.T, preferred_element_type=jnp.float32) + jnp.dot(grads[1], w_key.T, preferred_element_type=jnp.float32) + jnp.dot(grads[2], w_value.T, preferred_element_type=jnp.float32)).astype(jnp.bfloat16)
    grad_field = grad_hidden.reshape(frames, spatial, channels).astype(jnp.float32)
    return temporal_unmix(grad_field, conv_taps).astype(jnp.bfloat16)
```

```python
import functools
import math

import jax
import jax.numpy as jnp
from jax import lax
from jax.experimental import pallas as pl
from jax.experimental.pallas import tpu as pltpu
from jax.sharding import PartitionSpec as P

HEAD_DIM = 64
LANES = 128
BLOCK = 256
NT = (((1,), (1,)), ((), ()))
TN = (((0,), (0,)), ((), ()))


def iota(shape, dim):
    return lax.broadcasted_iota(jnp.int32, shape, dim)


def reorder_matrix(frames, toks, to_token_major):
    rows = frames * toks
    out_row = iota((rows, rows), 0)
    in_row = iota((rows, rows), 1)
    if to_token_major:
        source = (out_row % frames) * toks + out_row // frames
    else:
        source = (out_row % toks) * frames + out_row // toks
    return (in_row == source).astype(jnp.float32).astype(jnp.bfloat16)


def half_masks(rows):
    low = (iota((rows, LANES), 1) < HEAD_DIM).astype(jnp.float32)
    return low.astype(jnp.bfloat16), (1.0 - low).astype(jnp.bfloat16)


def split_pair(block, masks):
    return jnp.concatenate([block * masks[0], block * masks[1]], axis=0)


def compact(full, frames):
    token_of = iota((frames, LANES), 1) // frames
    kept = full[:frames]
    for tok in range(1, LANES // frames):
        kept = jnp.where(token_of == tok, full[tok * frames:(tok + 1) * frames], kept)
    return kept


def expand(kept, token_masks):
    return jnp.concatenate([kept * mask for mask in token_masks], axis=0)


def forward_kernel(me_ref, taps_ref, bias_ref, wq_ref, wk_ref, wv_ref, *refs, frames, toks, peers):
    blocks = refs[:peers]
    q_ref, k_ref, v_ref, prob_ref, source_ref, hidden_ref = refs[peers:]
    rows = frames * toks
    channels = hidden_ref.shape[1]
    part = rows // peers

    @pl.when(pl.program_id(0) == 0)
    def _():
        me = me_ref[0]
        for mask in range(peers):
            start = pl.multiple_of((me ^ mask) * part, part)
            source_ref[pl.ds(start, part), :] = blocks[mask][...].astype(jnp.float32)
        order = reorder_matrix(frames, toks, True)
        for col in range(0, channels, BLOCK):
            cols = slice(col, col + BLOCK)
            source = source_ref[:, cols]
            mixed = (
                taps_ref[0:1, cols] * pltpu.roll(source, toks, 0)
                + taps_ref[1:2, cols] * source
                + taps_ref[2:3, cols] * pltpu.roll(source, rows - toks, 0)
            )
            hidden = (source + mixed + bias_ref[:, cols]).astype(jnp.bfloat16)
            hidden_ref[:, cols] = jnp.dot(
                order, hidden, preferred_element_type=jnp.float32
            ).astype(jnp.bfloat16)

    hidden = hidden_ref[...]
    query = jnp.dot(hidden, wq_ref[...], preferred_element_type=jnp.float32).astype(jnp.bfloat16)
    key = jnp.dot(hidden, wk_ref[...], preferred_element_type=jnp.float32).astype(jnp.bfloat16)
    q_ref[...] = query
    k_ref[...] = key
    v_ref[...] = jnp.dot(hidden, wv_ref[...], preferred_element_type=jnp.float32).astype(jnp.bfloat16)
    masks = half_masks(LANES)
    inv_root = 1.0 / math.sqrt(HEAD_DIM)
    for pair in range(BLOCK // LANES):
        cols = slice(pair * LANES, (pair + 1) * LANES)
        for row in range(0, rows, LANES):
            full = lax.dot_general(
                split_pair(key[row:row + LANES, cols], masks), query[row:row + LANES, cols],
                NT, preferred_element_type=jnp.float32,
            )
            for head in range(2):
                scores = compact(full[head * LANES:(head + 1) * LANES], frames) * inv_root
                expo = jnp.exp(scores - jnp.max(scores, axis=0, keepdims=True))
                inverse = 1.0 / jnp.sum(expo, axis=0, keepdims=True)
                prob_ref[2 * pair + head, :, row:row + LANES] = expo * inverse


def backward_kernel(me_ref, taps_ref, wq_ref, wk_ref, wv_ref, q_ref, k_ref, v_ref, prob_ref,
                    *refs, frames, toks, peers):
    blocks = refs[:peers]
    outs = refs[peers:2 * peers]
    grad_ref, total_ref, result_ref = refs[2 * peers:]
    rows = frames * toks
    channels = grad_ref.shape[1] * grad_ref.shape[0]
    part = rows // peers
    step = pl.program_id(0)
    me = me_ref[0]

    @pl.when(step == 0)
    def _():
        for mask in range(peers):
            start = pl.multiple_of((me ^ mask) * part, part)
            result_ref[pl.ds(start, part), :] = blocks[mask][...]
        order = reorder_matrix(frames, toks, True)
        for index in range(channels // BLOCK):
            grad_ref[index] = jnp.dot(
                order, result_ref[:, index * BLOCK:(index + 1) * BLOCK],
                preferred_element_type=jnp.float32,
            ).astype(jnp.bfloat16)

    masks = half_masks(LANES)
    token_of = iota((frames, LANES), 1) // frames
    token_masks = [
        (token_of == tok).astype(jnp.float32).astype(jnp.bfloat16) for tok in range(LANES // frames)
    ]
    inv_root = 1.0 / math.sqrt(HEAD_DIM)
    grad = grad_ref[step]
    d_query, d_key, d_value = [], [], []
    for row in range(0, rows, LANES):
        row_q, row_k, row_v = [], [], []
        for pair in range(BLOCK // LANES):
            cols = slice(pair * LANES, (pair + 1) * LANES)
            here = slice(row, row + LANES)
            g_pair = grad[here, cols]
            full = lax.dot_general(
                split_pair(v_ref[here, cols], masks), g_pair, NT, preferred_element_type=jnp.float32
            )
            prob_wide, score_wide = [], []
            for head in range(2):
                prob = prob_ref[2 * pair + head, :, here]
                prob_low = prob.astype(jnp.bfloat16)
                grad_prob = compact(full[head * LANES:(head + 1) * LANES], frames)
                delta = jnp.sum(prob_low.astype(jnp.float32) * grad_prob, axis=0, keepdims=True)
                d_scores = (prob * (grad_prob - delta)).astype(jnp.bfloat16)
                prob_wide.append(expand(prob_low, token_masks))
                score_wide.append(expand(d_scores, token_masks))
            row_v.append(jnp.dot(
                jnp.concatenate(prob_wide, axis=1), split_pair(g_pair, masks),
                preferred_element_type=jnp.float32,
            ).astype(jnp.bfloat16))
            row_k.append((jnp.dot(
                jnp.concatenate(score_wide, axis=1), split_pair(q_ref[here, cols], masks),
                preferred_element_type=jnp.float32,
            ) * inv_root).astype(jnp.bfloat16))
            row_q.append((lax.dot_general(
                jnp.concatenate(score_wide, axis=0), split_pair(k_ref[here, cols], masks),
                TN, preferred_element_type=jnp.float32,
            ) * inv_root).astype(jnp.bfloat16))
        d_query.append(jnp.concatenate(row_q, axis=1))
        d_key.append(jnp.concatenate(row_k, axis=1))
        d_value.append(jnp.concatenate(row_v, axis=1))
    left = jnp.concatenate([jnp.concatenate(d, axis=0) for d in (d_query, d_key, d_value)], axis=1)
    right = jnp.concatenate([wq_ref[...], wk_ref[...], wv_ref[...]], axis=1)
    product = lax.dot_general(left, right, NT, preferred_element_type=jnp.float32)

    @pl.when(step == 0)
    def _():
        total_ref[...] = product

    @pl.when(step > 0)
    def _():
        total_ref[...] += product

    @pl.when(step == pl.num_programs(0) - 1)
    def _():
        order = reorder_matrix(frames, toks, False)
        for col in range(0, channels, BLOCK):
            cols = slice(col, col + BLOCK)
            source = jnp.dot(
                order, total_ref[:, cols].astype(jnp.bfloat16), preferred_element_type=jnp.float32
            )
            result_ref[:, cols] = (
                source
                + taps_ref[0:1, cols] * pltpu.roll(source, rows - toks, 0)
                + taps_ref[1:2, cols] * source
                + taps_ref[2:3, cols] * pltpu.roll(source, toks, 0)
            ).astype(jnp.bfloat16)
        for mask in range(peers):
            start = pl.multiple_of((me ^ mask) * part, part)
            outs[mask][...] = result_ref[pl.ds(start, part), :]


def exchange(parts, axis):
    peers = len(parts)
    return [parts[0]] + [
        lax.ppermute(parts[mask], axis, [(i, i ^ mask) for i in range(peers)])
        for mask in range(1, peers)
    ]


def butterfly_sum(value, axis):
    peers = lax.axis_size(axis)
    mask = 1
    while mask < peers:
        value = value + lax.ppermute(value, axis, [(i, i ^ mask) for i in range(peers)])
        mask *= 2
    return value


def shards(tokens, cotangent, w_query, w_key, w_value, conv_taps, conv_bias):
    frame_rows, tile_rows, channels = tokens.shape
    peers = lax.axis_size("orbit")
    me = lax.axis_index("orbit")
    frames = frame_rows * peers
    toks = tile_rows // peers
    rows = frames * toks
    part = frame_rows * toks
    spatial_all = tile_rows * lax.axis_size("tile")
    steps = channels // BLOCK

    def scatter(array):
        pieces = [
            lax.dynamic_slice_in_dim(array, (me ^ mask) * toks, toks, axis=1).reshape(part, channels)
            for mask in range(peers)
        ]
        return exchange(pieces, "orbit")

    grad_f = cotangent.astype(jnp.float32)
    energy = butterfly_sum(jnp.sum(grad_f * grad_f, axis=(1, 2)), "tile")
    token_parts = scatter(tokens)
    factor = lax.rsqrt(energy / (spatial_all * channels) + 1e-06)
    grad_out = (grad_f * factor[:, None, None]).astype(jnp.bfloat16)
    grad_parts = scatter(grad_out)

    me_arg = me.astype(jnp.int32).reshape(1)
    smem = pl.BlockSpec(memory_space=pltpu.SMEM)
    whole = lambda *shape: pl.BlockSpec(shape, lambda i: (0,) * len(shape))
    column = lambda height: pl.BlockSpec((height, BLOCK), lambda i: (0, i))
    heads = channels // HEAD_DIM
    step_heads = BLOCK // HEAD_DIM
    prob_spec = pl.BlockSpec((step_heads, frames, rows), lambda i: (i, 0, 0))
    sizes = dict(frames=frames, toks=toks, peers=peers)
    low = functools.partial(jax.ShapeDtypeStruct, dtype=jnp.bfloat16)
    query, key, value, prob = pl.pallas_call(
        functools.partial(forward_kernel, **sizes),
        grid=(steps,),
        in_specs=[smem, whole(3, channels), whole(1, channels)] + [column(channels)] * 3
        + [whole(part, channels)] * peers,
        out_specs=[column(rows)] * 3 + [prob_spec],
        out_shape=[low((rows, channels))] * 3
        + [jax.ShapeDtypeStruct((heads, frames, rows), jnp.float32)],
        scratch_shapes=[
            pltpu.VMEM((rows, channels), jnp.float32), pltpu.VMEM((rows, channels), jnp.bfloat16)
        ],
        name="forward",
    )(me_arg, conv_taps, conv_bias.reshape(1, channels), w_query, w_key, w_value, *token_parts)
    results = pl.pallas_call(
        functools.partial(backward_kernel, **sizes),
        grid=(steps,),
        in_specs=[smem, whole(3, channels)] + [column(channels)] * 3 + [column(rows)] * 3
        + [prob_spec] + [whole(part, channels)] * peers,
        out_specs=[whole(part, channels)] * peers,
        out_shape=[low((part, channels))] * peers,
        scratch_shapes=[
            pltpu.VMEM((steps, rows, BLOCK), jnp.bfloat16),
            pltpu.VMEM((rows, channels), jnp.float32),
            pltpu.VMEM((rows, channels), jnp.bfloat16),
        ],
        name="backward",
    )(me_arg, conv_taps, w_query, w_key, w_value, query, key, value, prob, *grad_parts)
    received = exchange(results, "orbit")
    output = jnp.zeros((frame_rows, tile_rows, channels), jnp.bfloat16)
    for mask in range(peers):
        output = lax.dynamic_update_slice_in_dim(
            output, received[mask].reshape(frame_rows, toks, channels), (me ^ mask) * toks, axis=1
        )
    return output


def solution(mesh):
    in_specs = (P("orbit", "tile", None), P("orbit", "tile", None), P(), P(), P(), P(), P())
    out_specs = P("orbit", "tile", None)
    return jax.shard_map(shards, mesh=mesh, in_specs=in_specs, out_specs=out_specs, check_vma=False)
```

```python
import functools
import math

import jax
import jax.numpy as jnp
from jax import lax
from jax.experimental import pallas as pl
from jax.experimental.pallas import tpu as pltpu
from jax.sharding import PartitionSpec as P


HEAD_DIM = 64
LANES = 128
BLOCK = 256
NT = (((1,), (1,)), ((), ()))
TN = (((0,), (0,)), ((), ()))


def iota(shape, dim):
    return lax.broadcasted_iota(jnp.int32, shape, dim)


def reorder_matrix(frames, toks, to_token_major):
    rows = frames * toks
    out_row = iota((rows, rows), 0)
    in_row = iota((rows, rows), 1)
    if to_token_major:
        source = (out_row % frames) * toks + out_row // frames
    else:
        source = (out_row % toks) * frames + out_row // toks
    return (in_row == source).astype(jnp.float32).astype(jnp.bfloat16)


def half_masks(rows):
    low = (iota((rows, LANES), 1) < HEAD_DIM).astype(jnp.float32)
    return low.astype(jnp.bfloat16), (1.0 - low).astype(jnp.bfloat16)


def split_pair(block, masks):
    return jnp.concatenate([block * masks[0], block * masks[1]], axis=0)


def compact(full, frames):
    token_of = iota((frames, LANES), 1) // frames
    kept = full[:frames]
    for tok in range(1, LANES // frames):
        kept = jnp.where(token_of == tok, full[tok * frames:(tok + 1) * frames], kept)
    return kept


def expand(kept, token_masks):
    return jnp.concatenate([kept * mask for mask in token_masks], axis=0)


def pack_kernel(me_ref, tokens_ref, cotangent_ref, *refs, peers):
    outs = refs[:peers // 2]
    energy_ref, held_ref, sems = refs[peers // 2:]
    me = me_ref[0]
    frame_rows = held_ref.shape[0]
    frame_copies = [
        pltpu.make_async_copy(cotangent_ref.at[frame], held_ref.at[frame], sems.at[peers + frame])
        for frame in range(frame_rows)
    ]
    copies = [
        pltpu.make_async_copy(
            tokens_ref.at[:, me ^ mask], outs[mask // 2].at[mask % 2], sems.at[mask]
        )
        for mask in range(peers)
    ]
    for copy in frame_copies + copies:
        copy.start()
    for frame in range(frame_rows):
        frame_copies[frame].wait()
        total = jnp.zeros(held_ref.shape[2:], jnp.float32)
        for group in range(peers):
            grad = held_ref[frame, group].astype(jnp.float32)
            total += grad * grad
        energy_ref[frame:frame + 1, :] = jnp.broadcast_to(
            jnp.sum(total, keepdims=True), (1, LANES)
        )
    for copy in copies:
        copy.wait()


def scale_kernel(me_ref, energy_ref, other_ref, cotangent_ref, *outs, peers, count):
    me = me_ref[0]
    factor = lax.rsqrt((energy_ref[...] + other_ref[...]) / count + 1e-06)
    frame_rows = cotangent_ref.shape[0]
    for mask in range(peers):
        for frame in range(frame_rows):
            grad = cotangent_ref[frame, me ^ mask].astype(jnp.float32)
            outs[mask // 2][mask % 2, frame] = (
                grad * factor[frame:frame + 1, :1]
            ).astype(jnp.bfloat16)


def load_kernel(*refs):
    count = len(refs) // 2
    sems = refs[-1]
    copies = [pltpu.make_async_copy(refs[i], refs[count + i], sems.at[i]) for i in range(count)]
    for copy in copies:
        copy.start()
    for copy in copies:
        copy.wait()


def place_kernel(me_ref, *refs, peers):
    blocks = refs[:peers]
    out_ref, sems = refs[peers:]
    me = me_ref[0]
    copies = [
        pltpu.make_async_copy(blocks[mask], out_ref.at[:, me ^ mask], sems.at[mask])
        for mask in range(peers)
    ]
    for copy in copies:
        copy.start()
    for copy in copies:
        copy.wait()


def block_of(blocks, mask):
    block = blocks[mask][...]
    return block[0] if mask % 2 == 0 else block


def forward_kernel(me_ref, taps_ref, bias_ref, wq_ref, wk_ref, wv_ref, *refs, frames, toks, peers):
    blocks = refs[:peers]
    q_ref, k_ref, v_ref, prob_ref, source_ref, hidden_ref = refs[peers:]
    rows, channels = hidden_ref.shape
    part = rows // peers
    me = me_ref[0]
    for mask in range(peers):
        start = pl.multiple_of((me ^ mask) * part, part)
        source_ref[pl.ds(start, part), :] = block_of(blocks, mask).astype(jnp.float32)
    order = reorder_matrix(frames, toks, True)
    for col in range(0, channels, BLOCK):
        cols = slice(col, col + BLOCK)
        source = source_ref[:, cols]
        mixed = (
            taps_ref[0:1, cols] * pltpu.roll(source, toks, 0)
            + taps_ref[1:2, cols] * source
            + taps_ref[2:3, cols] * pltpu.roll(source, rows - toks, 0)
        )
        hidden = (source + mixed + bias_ref[cols].reshape(1, BLOCK)).astype(jnp.bfloat16)
        hidden_ref[:, cols] = jnp.dot(
            order, hidden, preferred_element_type=jnp.float32
        ).astype(jnp.bfloat16)

    masks = half_masks(LANES)
    inv_root = 1.0 / math.sqrt(HEAD_DIM)
    for col in range(0, channels, BLOCK):
        block = slice(col, col + BLOCK)
        for weight_ref, out_ref in ((wq_ref, q_ref), (wk_ref, k_ref), (wv_ref, v_ref)):
            out_ref[:, block] = jnp.dot(
                hidden_ref[...], weight_ref[:, block], preferred_element_type=jnp.float32
            ).astype(jnp.bfloat16)
        for start in range(col, col + BLOCK, LANES):
            cols = slice(start, start + LANES)
            for row in range(0, rows, LANES):
                here = slice(row, row + LANES)
                full = lax.dot_general(
                    split_pair(k_ref[here, cols], masks), q_ref[here, cols],
                    NT, preferred_element_type=jnp.float32,
                )
                for head in range(2):
                    scores = compact(full[head * LANES:(head + 1) * LANES], frames) * inv_root
                    expo = jnp.exp(scores - jnp.max(scores, axis=0, keepdims=True))
                    inverse = 1.0 / jnp.sum(expo, axis=0, keepdims=True)
                    prob_ref[start // HEAD_DIM + head, :, here] = expo * inverse


def backward_kernel(me_ref, taps_ref, wq_ref, wk_ref, wv_ref, q_ref, k_ref, v_ref, prob_ref,
                    *refs, frames, toks, peers):
    blocks = refs[:peers]
    outs = refs[peers:2 * peers]
    grad_ref, left_ref, result_ref = refs[2 * peers:]
    rows, channels = grad_ref.shape
    part = rows // peers
    me = me_ref[0]
    for mask in range(peers):
        start = pl.multiple_of((me ^ mask) * part, part)
        result_ref[pl.ds(start, part), :] = block_of(blocks, mask)
    order = reorder_matrix(frames, toks, True)
    for col in range(0, channels, BLOCK):
        cols = slice(col, col + BLOCK)
        grad_ref[:, cols] = jnp.dot(
            order, result_ref[:, cols], preferred_element_type=jnp.float32
        ).astype(jnp.bfloat16)

    masks = half_masks(LANES)
    token_of = iota((frames, LANES), 1) // frames
    token_masks = [
        (token_of == tok).astype(jnp.float32).astype(jnp.bfloat16) for tok in range(LANES // frames)
    ]
    inv_root = 1.0 / math.sqrt(HEAD_DIM)
    for start in range(0, channels, LANES):
        cols = slice(start, start + LANES)
        for row in range(0, rows, LANES):
            here = slice(row, row + LANES)
            g_pair = grad_ref[here, cols]
            full = lax.dot_general(
                split_pair(v_ref[here, cols], masks), g_pair, NT, preferred_element_type=jnp.float32
            )
            prob_wide, score_wide = [], []
            for head in range(2):
                prob = prob_ref[start // HEAD_DIM + head, :, here]
                prob_low = prob.astype(jnp.bfloat16)
                grad_prob = compact(full[head * LANES:(head + 1) * LANES], frames)
                delta = jnp.sum(prob_low.astype(jnp.float32) * grad_prob, axis=0, keepdims=True)
                d_scores = (prob * (grad_prob - delta)).astype(jnp.bfloat16)
                prob_wide.append(expand(prob_low, token_masks))
                score_wide.append(expand(d_scores, token_masks))
            left_ref[0, here, cols] = (lax.dot_general(
                jnp.concatenate(score_wide, axis=0), split_pair(k_ref[here, cols], masks),
                TN, preferred_element_type=jnp.float32,
            ) * inv_root).astype(jnp.bfloat16)
            left_ref[1, here, cols] = (jnp.dot(
                jnp.concatenate(score_wide, axis=1), split_pair(q_ref[here, cols], masks),
                preferred_element_type=jnp.float32,
            ) * inv_root).astype(jnp.bfloat16)
            left_ref[2, here, cols] = jnp.dot(
                jnp.concatenate(prob_wide, axis=1), split_pair(g_pair, masks),
                preferred_element_type=jnp.float32,
            ).astype(jnp.bfloat16)

    order = reorder_matrix(frames, toks, False)
    for col in range(0, channels, BLOCK):
        cols = slice(col, col + BLOCK)
        total = sum(
            lax.dot_general(left_ref[index], weight_ref[cols, :], NT, preferred_element_type=jnp.float32)
            for index, weight_ref in enumerate((wq_ref, wk_ref, wv_ref))
        )
        source = jnp.dot(order, total.astype(jnp.bfloat16), preferred_element_type=jnp.float32)
        result_ref[:, cols] = (
            source
            + taps_ref[0:1, cols] * pltpu.roll(source, rows - toks, 0)
            + taps_ref[1:2, cols] * source
            + taps_ref[2:3, cols] * pltpu.roll(source, toks, 0)
        ).astype(jnp.bfloat16)
    for mask in range(peers):
        start = pl.multiple_of((me ^ mask) * part, part)
        outs[mask][...] = result_ref[pl.ds(start, part), :]


def swap(value, axis, mask):
    return lax.ppermute(value, axis, [(i, i ^ mask) for i in range(lax.axis_size(axis))])


def grant(mebibytes):
    return pltpu.CompilerParams(vmem_limit_bytes=mebibytes << 20)


def on_chip(value):
    return pltpu.with_memory_space_constraint(value, pltpu.VMEM)


def off_chip(value):
    return pltpu.with_memory_space_constraint(value, pltpu.HBM)


def far_first(peers):
    return sorted(range(1, peers), key=lambda mask: (-bin(mask >> 1).count("1"), -mask))


def gather_tokens(sent):
    peers = lax.axis_size("orbit")
    _, frame_rows, toks, channels = sent[0].shape
    parts = [sent[0]] + [None] * (peers // 2 - 1)
    for mask in far_first(peers):
        if mask % 2 == 0:
            parts[mask // 2] = swap(sent[mask // 2], "orbit", mask)
    blocks = []
    for chip in range(peers // 2):
        pair = parts[chip].reshape(2, frame_rows * toks, channels)
        mine = pair[1]
        blocks += [pair, swap(mine, "orbit", 1)]
    return blocks


def spread_frames(blocks):
    peers = len(blocks)
    received = [blocks[0]] + [None] * (peers - 1)
    for mask in far_first(peers):
        received[mask] = swap(blocks[mask], "orbit", mask)
    return received


def tile_sum(value):
    mask = 1
    other = jnp.zeros_like(value)
    while mask < lax.axis_size("tile"):
        value = value + other if mask > 1 else value
        other = swap(value, "tile", mask)
        mask *= 2
    return value, other


def body(tokens, cotangent, w_query, w_key, w_value, conv_taps, conv_bias):
    frame_rows, tile_rows, channels = tokens.shape
    peers = lax.axis_size("orbit")
    me = lax.axis_index("orbit")
    frames = frame_rows * peers
    toks = tile_rows // peers
    rows = frames * toks
    part = frame_rows * toks
    spatial_all = tile_rows * lax.axis_size("tile")
    heads = channels // HEAD_DIM
    me_arg = me.astype(jnp.int32).reshape(1)
    smem = pl.BlockSpec(memory_space=pltpu.SMEM)
    vmem = pl.BlockSpec(memory_space=pltpu.VMEM)
    hbm = pl.BlockSpec(memory_space=pltpu.HBM)
    low = functools.partial(pltpu.VMEM, dtype=jnp.bfloat16)
    sent_shape = low((2, frame_rows, toks, channels))
    split = (frame_rows, peers, toks, channels)

    *sent_tokens, energy, held = pl.pallas_call(
        functools.partial(pack_kernel, peers=peers),
        in_specs=[smem, hbm, hbm],
        out_specs=[vmem] * (peers // 2 + 2),
        out_shape=[sent_shape] * (peers // 2)
        + [pltpu.VMEM((frame_rows, LANES), jnp.float32), low(split)],
        scratch_shapes=[pltpu.SemaphoreType.DMA((peers + frame_rows,))],
        compiler_params=grant(8),
        name="pack",
    )(me_arg, off_chip(tokens.reshape(split)), off_chip(cotangent.reshape(split)))
    energy_here, energy_there = tile_sum(energy)
    token_blocks = gather_tokens(sent_tokens)
    sent_grads = pl.pallas_call(
        functools.partial(scale_kernel, peers=peers, count=spatial_all * channels),
        in_specs=[smem, vmem, vmem, vmem],
        out_specs=[vmem] * (peers // 2),
        out_shape=[sent_shape] * (peers // 2),
        compiler_params=grant(8),
        name="scale",
    )(me_arg, on_chip(energy_here), on_chip(energy_there), on_chip(held))
    grad_blocks = gather_tokens(sent_grads)

    parameters = (conv_taps, conv_bias, w_query, w_key, w_value)
    conv_taps, conv_bias, *weights = map(on_chip, pl.pallas_call(
        load_kernel,
        in_specs=[hbm] * len(parameters),
        out_specs=[vmem] * len(parameters),
        out_shape=[pltpu.VMEM(value.shape, value.dtype) for value in parameters],
        scratch_shapes=[pltpu.SemaphoreType.DMA((len(parameters),))],
        compiler_params=grant(4),
        name="load",
    )(*map(off_chip, parameters)))
    sizes = dict(frames=frames, toks=toks, peers=peers)
    query, key, value, prob = pl.pallas_call(
        functools.partial(forward_kernel, **sizes),
        in_specs=[smem] + [vmem] * (5 + peers),
        out_specs=[vmem] * 4,
        out_shape=[low((rows, channels))] * 3 + [pltpu.VMEM((heads, frames, rows), jnp.float32)],
        scratch_shapes=[
            pltpu.VMEM((rows, channels), jnp.float32), pltpu.VMEM((rows, channels), jnp.bfloat16)
        ],
        compiler_params=grant(20),
        name="forward",
    )(me_arg, conv_taps, conv_bias, *weights, *map(on_chip, token_blocks))
    results = pl.pallas_call(
        functools.partial(backward_kernel, **sizes),
        in_specs=[smem] + [vmem] * (8 + peers),
        out_specs=[vmem] * peers,
        out_shape=[low((part, channels))] * peers,
        scratch_shapes=[
            pltpu.VMEM((rows, channels), jnp.bfloat16),
            pltpu.VMEM((3, rows, channels), jnp.bfloat16),
            pltpu.VMEM((rows, channels), jnp.bfloat16),
        ],
        compiler_params=grant(20),
        name="backward",
    )(me_arg, conv_taps, *weights, *map(on_chip, (query, key, value, prob)), *map(on_chip, grad_blocks))
    received = [block.reshape(frame_rows, toks, channels) for block in spread_frames(results)]
    output = pl.pallas_call(
        functools.partial(place_kernel, peers=peers),
        in_specs=[smem] + [vmem] * peers,
        out_specs=hbm,
        out_shape=jax.ShapeDtypeStruct(split, jnp.bfloat16),
        scratch_shapes=[pltpu.SemaphoreType.DMA((peers,))],
        compiler_params=grant(4),
        name="place",
    )(me_arg, *map(on_chip, received))
    return output.reshape(frame_rows, tile_rows, channels)


def solution(mesh):
    in_specs = (P("orbit", "tile", None), P("orbit", "tile", None), P(), P(), P(), P(), P())
    out_specs = P("orbit", "tile", None)
    return jax.shard_map(body, mesh=mesh, in_specs=in_specs, out_specs=out_specs, check_vma=False)
```

```python
import functools
import math

import jax
import jax.numpy as jnp
from jax import lax
from jax.experimental import pallas as pl
from jax.experimental.pallas import tpu as pltpu
from jax.sharding import PartitionSpec as P


HEAD_DIM = 64
LANES = 128
BLOCK = 256
NT = (((1,), (1,)), ((), ()))
TN = (((0,), (0,)), ((), ()))


def iota(shape, dim):
    return lax.broadcasted_iota(jnp.int32, shape, dim)


def reorder_matrix(frames, toks, to_token_major):
    rows = frames * toks
    out_row = iota((rows, rows), 0)
    in_row = iota((rows, rows), 1)
    if to_token_major:
        source = (out_row % frames) * toks + out_row // frames
    else:
        source = (out_row % toks) * frames + out_row // toks
    return (in_row == source).astype(jnp.float32).astype(jnp.bfloat16)


def half_masks(rows):
    low = (iota((rows, LANES), 1) < HEAD_DIM).astype(jnp.float32)
    return low.astype(jnp.bfloat16), (1.0 - low).astype(jnp.bfloat16)


def split_pair(block, masks):
    return jnp.concatenate([block * masks[0], block * masks[1]], axis=0)


def compact(full, frames):
    token_of = iota((frames, LANES), 1) // frames
    kept = full[:frames]
    for tok in range(1, LANES // frames):
        kept = jnp.where(token_of == tok, full[tok * frames:(tok + 1) * frames], kept)
    return kept


def expand(kept, token_masks):
    return jnp.concatenate([kept * mask for mask in token_masks], axis=0)


def pack_kernel(me_ref, tokens_ref, *refs):
    outs, sems = refs[:-1], refs[-1]
    me = me_ref[0]
    copies = [
        pltpu.make_async_copy(
            tokens_ref.at[:, me ^ mask], outs[mask // 2].at[mask % 2], sems.at[mask]
        )
        for mask in range(2 * len(outs))
    ]
    for copy in copies:
        copy.start()
    for copy in copies:
        copy.wait()


def energy_kernel(cotangent_ref, energy_ref, held_ref, sems):
    frame_rows, groups = held_ref.shape[:2]
    copies = [
        pltpu.make_async_copy(cotangent_ref.at[frame], held_ref.at[frame], sems.at[frame])
        for frame in range(frame_rows)
    ]
    for copy in copies:
        copy.start()
    for frame in range(frame_rows):
        copies[frame].wait()
        total = jnp.zeros(held_ref.shape[2:], jnp.float32)
        for group in range(groups):
            grad = held_ref[frame, group].astype(jnp.float32)
            total += grad * grad
        energy_ref[frame:frame + 1, :] = jnp.broadcast_to(
            jnp.sum(total, keepdims=True), (1, LANES)
        )


def scale_kernel(me_ref, held_ref, *refs, peers, count):
    energies, outs = refs[:-(peers // 2)], refs[-(peers // 2):]
    me = me_ref[0]
    factor = lax.rsqrt(sum(energy[...] for energy in energies) / count + 1e-06)
    frame_rows = held_ref.shape[0]
    for mask in range(peers):
        for frame in range(frame_rows):
            grad = held_ref[frame, me ^ mask].astype(jnp.float32)
            outs[mask // 2][mask % 2, frame] = (
                grad * factor[frame:frame + 1, :1]
            ).astype(jnp.bfloat16)


def place_kernel(me_ref, *refs, peers):
    blocks = refs[:peers]
    out_ref, sems = refs[peers:]
    me = me_ref[0]
    copies = [
        pltpu.make_async_copy(blocks[mask], out_ref.at[:, me ^ mask], sems.at[mask])
        for mask in range(peers)
    ]
    for copy in copies:
        copy.start()
    for copy in copies:
        copy.wait()


def block_of(blocks, mask):
    block = blocks[mask][...]
    return block[0] if mask % 2 == 0 else block


def forward_kernel(me_ref, taps_ref, bias_ref, wq_ref, wk_ref, wv_ref, *refs, frames, toks, peers):
    blocks = refs[:peers]
    q_ref, k_ref, v_ref, prob_ref, source_ref, hidden_ref = refs[peers:]
    rows, channels = hidden_ref.shape
    part = rows // peers
    me = me_ref[0]
    for mask in range(peers):
        start = pl.multiple_of((me ^ mask) * part, part)
        source_ref[pl.ds(start, part), :] = block_of(blocks, mask).astype(jnp.float32)
    order = reorder_matrix(frames, toks, True)
    for col in range(0, channels, BLOCK):
        cols = slice(col, col + BLOCK)
        source = source_ref[:, cols]
        mixed = (
            taps_ref[0:1, cols] * pltpu.roll(source, toks, 0)
            + taps_ref[1:2, cols] * source
            + taps_ref[2:3, cols] * pltpu.roll(source, rows - toks, 0)
        )
        hidden = (source + mixed + bias_ref[cols].reshape(1, BLOCK)).astype(jnp.bfloat16)
        hidden_ref[:, cols] = jnp.dot(
            order, hidden, preferred_element_type=jnp.float32
        ).astype(jnp.bfloat16)

    masks = half_masks(LANES)
    inv_root = 1.0 / math.sqrt(HEAD_DIM)
    for col in range(0, channels, BLOCK):
        block = slice(col, col + BLOCK)
        for weight_ref, out_ref in ((wq_ref, q_ref), (wk_ref, k_ref), (wv_ref, v_ref)):
            out_ref[:, block] = jnp.dot(
                hidden_ref[...], weight_ref[:, block], preferred_element_type=jnp.float32
            ).astype(jnp.bfloat16)
        for start in range(col, col + BLOCK, LANES):
            cols = slice(start, start + LANES)
            for row in range(0, rows, LANES):
                here = slice(row, row + LANES)
                full = lax.dot_general(
                    split_pair(k_ref[here, cols], masks), q_ref[here, cols],
                    NT, preferred_element_type=jnp.float32,
                )
                for head in range(2):
                    scores = compact(full[head * LANES:(head + 1) * LANES], frames) * inv_root
                    expo = jnp.exp(scores - jnp.max(scores, axis=0, keepdims=True))
                    inverse = 1.0 / jnp.sum(expo, axis=0, keepdims=True)
                    prob_ref[start // HEAD_DIM + head, :, here] = expo * inverse


def backward_kernel(me_ref, taps_ref, wq_ref, wk_ref, wv_ref, q_ref, k_ref, v_ref, prob_ref,
                    *refs, frames, toks, peers):
    blocks = refs[:peers]
    outs = refs[peers:2 * peers]
    grad_ref, left_ref, result_ref = refs[2 * peers:]
    rows, channels = grad_ref.shape
    part = rows // peers
    me = me_ref[0]
    for mask in range(peers):
        start = pl.multiple_of((me ^ mask) * part, part)
        result_ref[pl.ds(start, part), :] = block_of(blocks, mask)
    order = reorder_matrix(frames, toks, True)
    for col in range(0, channels, BLOCK):
        cols = slice(col, col + BLOCK)
        grad_ref[:, cols] = jnp.dot(
            order, result_ref[:, cols], preferred_element_type=jnp.float32
        ).astype(jnp.bfloat16)

    masks = half_masks(LANES)
    token_of = iota((frames, LANES), 1) // frames
    token_masks = [
        (token_of == tok).astype(jnp.float32).astype(jnp.bfloat16) for tok in range(LANES // frames)
    ]
    inv_root = 1.0 / math.sqrt(HEAD_DIM)
    for start in range(0, channels, LANES):
        cols = slice(start, start + LANES)
        for row in range(0, rows, LANES):
            here = slice(row, row + LANES)
            g_pair = grad_ref[here, cols]
            full = lax.dot_general(
                split_pair(v_ref[here, cols], masks), g_pair, NT, preferred_element_type=jnp.float32
            )
            prob_wide, score_wide = [], []
            for head in range(2):
                prob = prob_ref[start // HEAD_DIM + head, :, here]
                prob_low = prob.astype(jnp.bfloat16)
                grad_prob = compact(full[head * LANES:(head + 1) * LANES], frames)
                delta = jnp.sum(prob_low.astype(jnp.float32) * grad_prob, axis=0, keepdims=True)
                d_scores = (prob * (grad_prob - delta)).astype(jnp.bfloat16)
                prob_wide.append(expand(prob_low, token_masks))
                score_wide.append(expand(d_scores, token_masks))
            left_ref[0, here, cols] = (lax.dot_general(
                jnp.concatenate(score_wide, axis=0), split_pair(k_ref[here, cols], masks),
                TN, preferred_element_type=jnp.float32,
            ) * inv_root).astype(jnp.bfloat16)
            left_ref[1, here, cols] = (jnp.dot(
                jnp.concatenate(score_wide, axis=1), split_pair(q_ref[here, cols], masks),
                preferred_element_type=jnp.float32,
            ) * inv_root).astype(jnp.bfloat16)
            left_ref[2, here, cols] = jnp.dot(
                jnp.concatenate(prob_wide, axis=1), split_pair(g_pair, masks),
                preferred_element_type=jnp.float32,
            ).astype(jnp.bfloat16)

    order = reorder_matrix(frames, toks, False)
    for col in range(0, channels, BLOCK):
        cols = slice(col, col + BLOCK)
        total = sum(
            lax.dot_general(left_ref[index], weight_ref[cols, :], NT, preferred_element_type=jnp.float32)
            for index, weight_ref in enumerate((wq_ref, wk_ref, wv_ref))
        )
        source = jnp.dot(order, total.astype(jnp.bfloat16), preferred_element_type=jnp.float32)
        result_ref[:, cols] = (
            source
            + taps_ref[0:1, cols] * pltpu.roll(source, rows - toks, 0)
            + taps_ref[1:2, cols] * source
            + taps_ref[2:3, cols] * pltpu.roll(source, toks, 0)
        ).astype(jnp.bfloat16)
    for mask in range(peers):
        start = pl.multiple_of((me ^ mask) * part, part)
        outs[mask][...] = result_ref[pl.ds(start, part), :]


def swap(value, axis, mask):
    return lax.ppermute(value, axis, [(i, i ^ mask) for i in range(lax.axis_size(axis))])


def grant(mebibytes):
    return pltpu.CompilerParams(vmem_limit_bytes=mebibytes << 20)


def on_chip(value):
    return pltpu.with_memory_space_constraint(value, pltpu.VMEM)


def off_chip(value):
    return pltpu.with_memory_space_constraint(value, pltpu.HBM)


def far_first(peers):
    return sorted(range(1, peers), key=lambda mask: (-bin(mask >> 1).count("1"), -mask))


def gather_tokens(sent):
    peers = lax.axis_size("orbit")
    _, frame_rows, toks, channels = sent[0].shape
    parts = [sent[0]] + [None] * (peers // 2 - 1)
    for mask in far_first(peers):
        if mask % 2 == 0:
            parts[mask // 2] = swap(sent[mask // 2], "orbit", mask)
    blocks = []
    for chip in range(peers // 2):
        pair = parts[chip].reshape(2, frame_rows * toks, channels)
        mine = pair[1]
        blocks += [pair, swap(mine, "orbit", 1)]
    return blocks


def spread_frames(blocks):
    peers = len(blocks)
    received = [blocks[0]] + [None] * (peers - 1)
    for mask in far_first(peers):
        received[mask] = swap(blocks[mask], "orbit", mask)
    return received


def tile_masks(peers):
    stages, stride = [], 1
    while stride < peers:
        radix = min(4, peers // stride)
        stages.append([stride * step for step in range(radix - 1, 0, -1)])
        stride *= radix
    return stages


def tile_terms(value):
    terms = [value]
    for masks in tile_masks(lax.axis_size("tile")):
        value = sum(terms[1:], terms[0])
        terms = [value] + [swap(value, "tile", mask) for mask in masks]
    return terms


def body(tokens, cotangent, w_query, w_key, w_value, conv_taps, conv_bias):
    frame_rows, tile_rows, channels = tokens.shape
    peers = lax.axis_size("orbit")
    me = lax.axis_index("orbit")
    frames = frame_rows * peers
    toks = tile_rows // peers
    rows = frames * toks
    part = frame_rows * toks
    spatial_all = tile_rows * lax.axis_size("tile")
    heads = channels // HEAD_DIM
    me_arg = me.astype(jnp.int32).reshape(1)
    smem = pl.BlockSpec(memory_space=pltpu.SMEM)
    vmem = pl.BlockSpec(memory_space=pltpu.VMEM)
    hbm = pl.BlockSpec(memory_space=pltpu.HBM)
    low = functools.partial(pltpu.VMEM, dtype=jnp.bfloat16)
    sent_shape = low((2, frame_rows, toks, channels))
    split = (frame_rows, peers, toks, channels)

    sent_tokens = pl.pallas_call(
        pack_kernel,
        in_specs=[smem, hbm],
        out_specs=[vmem] * (peers // 2),
        out_shape=[sent_shape] * (peers // 2),
        scratch_shapes=[pltpu.SemaphoreType.DMA((peers,))],
        compiler_params=grant(4),
        name="pack",
    )(me_arg, off_chip(tokens.reshape(split)))
    token_blocks = gather_tokens(sent_tokens)
    energy, held = pl.pallas_call(
        energy_kernel,
        in_specs=[hbm],
        out_specs=[vmem] * 2,
        out_shape=[pltpu.VMEM((frame_rows, LANES), jnp.float32), low(split)],
        scratch_shapes=[pltpu.SemaphoreType.DMA((frame_rows,))],
        compiler_params=grant(4),
        name="energy",
    )(off_chip(cotangent.reshape(split)))
    terms = tile_terms(energy)
    sent_grads = pl.pallas_call(
        functools.partial(scale_kernel, peers=peers, count=spatial_all * channels),
        in_specs=[smem] + [vmem] * (1 + len(terms)),
        out_specs=[vmem] * (peers // 2),
        out_shape=[sent_shape] * (peers // 2),
        compiler_params=grant(8),
        cost_estimate=pl.CostEstimate(flops=1 << 34, bytes_accessed=1 << 25, transcendentals=0),
        name="scale",
    )(me_arg, on_chip(held), *map(on_chip, terms))
    grad_blocks = gather_tokens(sent_grads)

    weights = (w_query, w_key, w_value)
    sizes = dict(frames=frames, toks=toks, peers=peers)
    query, key, value, prob = pl.pallas_call(
        functools.partial(forward_kernel, **sizes),
        in_specs=[smem] + [vmem] * (5 + peers),
        out_specs=[vmem] * 4,
        out_shape=[low((rows, channels))] * 3 + [pltpu.VMEM((heads, frames, rows), jnp.float32)],
        scratch_shapes=[
            pltpu.VMEM((rows, channels), jnp.float32), pltpu.VMEM((rows, channels), jnp.bfloat16)
        ],
        compiler_params=grant(20),
        name="forward",
    )(me_arg, conv_taps, conv_bias, *weights, *map(on_chip, token_blocks))
    results = pl.pallas_call(
        functools.partial(backward_kernel, **sizes),
        in_specs=[smem] + [vmem] * (8 + peers),
        out_specs=[vmem] * peers,
        out_shape=[low((part, channels))] * peers,
        scratch_shapes=[
            pltpu.VMEM((rows, channels), jnp.bfloat16),
            pltpu.VMEM((3, rows, channels), jnp.bfloat16),
            pltpu.VMEM((rows, channels), jnp.bfloat16),
        ],
        compiler_params=grant(20),
        name="backward",
    )(me_arg, conv_taps, *weights, *map(on_chip, (query, key, value, prob)), *map(on_chip, grad_blocks))
    received = [block.reshape(frame_rows, toks, channels) for block in spread_frames(results)]
    output = pl.pallas_call(
        functools.partial(place_kernel, peers=peers),
        in_specs=[smem] + [vmem] * peers,
        out_specs=hbm,
        out_shape=jax.ShapeDtypeStruct(split, jnp.bfloat16),
        scratch_shapes=[pltpu.SemaphoreType.DMA((peers,))],
        compiler_params=grant(4),
        name="place",
    )(me_arg, *map(on_chip, received))
    return output.reshape(frame_rows, tile_rows, channels)


def solution(mesh):
    in_specs = (P("orbit", "tile", None), P("orbit", "tile", None), P(), P(), P(), P(), P())
    out_specs = P("orbit", "tile", None)
    return jax.shard_map(body, mesh=mesh, in_specs=in_specs, out_specs=out_specs, check_vma=False)
```

```python
import functools
import math

import jax
import jax.numpy as jnp
from jax import lax
from jax.experimental import pallas as pl
from jax.experimental.pallas import tpu as pltpu
from jax.sharding import PartitionSpec as P


HEAD_DIM = 64
LANES = 128
BLOCK = 256
NT = (((1,), (1,)), ((), ()))
TN = (((0,), (0,)), ((), ()))


def iota(shape, dim):
    return lax.broadcasted_iota(jnp.int32, shape, dim)


def reorder_matrix(frames, toks, to_token_major):
    rows = frames * toks
    out_row = iota((rows, rows), 0)
    in_row = iota((rows, rows), 1)
    if to_token_major:
        source = (out_row % frames) * toks + out_row // frames
    else:
        source = (out_row % toks) * frames + out_row // toks
    return (in_row == source).astype(jnp.float32).astype(jnp.bfloat16)


def half_masks(rows):
    low = (iota((rows, LANES), 1) < HEAD_DIM).astype(jnp.float32)
    return low.astype(jnp.bfloat16), (1.0 - low).astype(jnp.bfloat16)


def split_pair(block, masks):
    return jnp.concatenate([block * masks[0], block * masks[1]], axis=0)


def compact(full, frames):
    token_of = iota((frames, LANES), 1) // frames
    kept = full[:frames]
    for tok in range(1, LANES // frames):
        kept = jnp.where(token_of == tok, full[tok * frames:(tok + 1) * frames], kept)
    return kept


def expand(kept, token_masks):
    return jnp.concatenate([kept * mask for mask in token_masks], axis=0)


def pack_kernel(me_ref, tokens_ref, cotangent_ref, *refs, peers):
    outs = refs[:peers // 2]
    energy_ref, held_ref, sems = refs[peers // 2:]
    me = me_ref[0]
    frame_rows = held_ref.shape[0]
    frame_copies = [
        pltpu.make_async_copy(cotangent_ref.at[frame], held_ref.at[frame], sems.at[peers + frame])
        for frame in range(frame_rows)
    ]
    copies = [
        pltpu.make_async_copy(
            tokens_ref.at[:, me ^ mask], outs[mask // 2].at[mask % 2], sems.at[mask]
        )
        for mask in range(peers)
    ]
    for copy in frame_copies + copies:
        copy.start()
    for frame in range(frame_rows):
        frame_copies[frame].wait()
        total = jnp.zeros(held_ref.shape[2:], jnp.float32)
        for group in range(peers):
            grad = held_ref[frame, group].astype(jnp.float32)
            total += grad * grad
        energy_ref[frame:frame + 1, :] = jnp.broadcast_to(
            jnp.sum(total, keepdims=True), (1, LANES)
        )
    for copy in copies:
        copy.wait()


def scale_kernel(me_ref, held_ref, *refs, peers, count):
    energies, outs = refs[:-(peers // 2)], refs[-(peers // 2):]
    me = me_ref[0]
    factor = lax.rsqrt(sum(energy[...] for energy in energies) / count + 1e-06)
    frame_rows = held_ref.shape[0]
    for mask in range(peers):
        for frame in range(frame_rows):
            grad = held_ref[frame, me ^ mask].astype(jnp.float32)
            outs[mask // 2][mask % 2, frame] = (
                grad * factor[frame:frame + 1, :1]
            ).astype(jnp.bfloat16)


def place_kernel(me_ref, *refs, peers):
    blocks = refs[:peers]
    out_ref, sems = refs[peers:]
    me = me_ref[0]
    copies = [
        pltpu.make_async_copy(blocks[mask], out_ref.at[:, me ^ mask], sems.at[mask])
        for mask in range(peers)
    ]
    for copy in copies:
        copy.start()
    for copy in copies:
        copy.wait()


def block_of(blocks, mask):
    block = blocks[mask][...]
    return block[0] if mask % 2 == 0 else block


def forward_kernel(me_ref, taps_ref, bias_ref, wq_ref, wk_ref, wv_ref, *refs, frames, toks, peers):
    blocks = refs[:peers]
    q_ref, k_ref, v_ref, prob_ref, source_ref, hidden_ref = refs[peers:]
    rows, channels = hidden_ref.shape
    part = rows // peers
    me = me_ref[0]
    for mask in range(peers):
        start = pl.multiple_of((me ^ mask) * part, part)
        source_ref[pl.ds(start, part), :] = block_of(blocks, mask).astype(jnp.float32)
    order = reorder_matrix(frames, toks, True)
    for col in range(0, channels, BLOCK):
        cols = slice(col, col + BLOCK)
        source = source_ref[:, cols]
        mixed = (
            taps_ref[0:1, cols] * pltpu.roll(source, toks, 0)
            + taps_ref[1:2, cols] * source
            + taps_ref[2:3, cols] * pltpu.roll(source, rows - toks, 0)
        )
        hidden = (source + mixed + bias_ref[cols].reshape(1, BLOCK)).astype(jnp.bfloat16)
        hidden_ref[:, cols] = jnp.dot(
            order, hidden, preferred_element_type=jnp.float32
        ).astype(jnp.bfloat16)

    masks = half_masks(LANES)
    inv_root = 1.0 / math.sqrt(HEAD_DIM)
    for col in range(0, channels, BLOCK):
        block = slice(col, col + BLOCK)
        for weight_ref, out_ref in ((wq_ref, q_ref), (wk_ref, k_ref), (wv_ref, v_ref)):
            out_ref[:, block] = jnp.dot(
                hidden_ref[...], weight_ref[:, block], preferred_element_type=jnp.float32
            ).astype(jnp.bfloat16)
        for start in range(col, col + BLOCK, LANES):
            cols = slice(start, start + LANES)
            for row in range(0, rows, LANES):
                here = slice(row, row + LANES)
                full = lax.dot_general(
                    split_pair(k_ref[here, cols], masks), q_ref[here, cols],
                    NT, preferred_element_type=jnp.float32,
                )
                for head in range(2):
                    scores = compact(full[head * LANES:(head + 1) * LANES], frames) * inv_root
                    expo = jnp.exp(scores - jnp.max(scores, axis=0, keepdims=True))
                    inverse = 1.0 / jnp.sum(expo, axis=0, keepdims=True)
                    prob_ref[start // HEAD_DIM + head, :, here] = expo * inverse


def backward_kernel(me_ref, taps_ref, wq_ref, wk_ref, wv_ref, q_ref, k_ref, v_ref, prob_ref,
                    *refs, frames, toks, peers):
    blocks = refs[:peers]
    outs = refs[peers:2 * peers]
    grad_ref, left_ref, result_ref = refs[2 * peers:]
    rows, channels = grad_ref.shape
    part = rows // peers
    me = me_ref[0]
    for mask in range(peers):
        start = pl.multiple_of((me ^ mask) * part, part)
        result_ref[pl.ds(start, part), :] = block_of(blocks, mask)
    order = reorder_matrix(frames, toks, True)
    for col in range(0, channels, BLOCK):
        cols = slice(col, col + BLOCK)
        grad_ref[:, cols] = jnp.dot(
            order, result_ref[:, cols], preferred_element_type=jnp.float32
        ).astype(jnp.bfloat16)

    masks = half_masks(LANES)
    token_of = iota((frames, LANES), 1) // frames
    token_masks = [
        (token_of == tok).astype(jnp.float32).astype(jnp.bfloat16) for tok in range(LANES // frames)
    ]
    inv_root = 1.0 / math.sqrt(HEAD_DIM)
    for start in range(0, channels, LANES):
        cols = slice(start, start + LANES)
        for row in range(0, rows, LANES):
            here = slice(row, row + LANES)
            g_pair = grad_ref[here, cols]
            full = lax.dot_general(
                split_pair(v_ref[here, cols], masks), g_pair, NT, preferred_element_type=jnp.float32
            )
            prob_wide, score_wide = [], []
            for head in range(2):
                prob = prob_ref[start // HEAD_DIM + head, :, here]
                prob_low = prob.astype(jnp.bfloat16)
                grad_prob = compact(full[head * LANES:(head + 1) * LANES], frames)
                delta = jnp.sum(prob_low.astype(jnp.float32) * grad_prob, axis=0, keepdims=True)
                d_scores = (prob * (grad_prob - delta)).astype(jnp.bfloat16)
                prob_wide.append(expand(prob_low, token_masks))
                score_wide.append(expand(d_scores, token_masks))
            left_ref[0, here, cols] = (lax.dot_general(
                jnp.concatenate(score_wide, axis=0), split_pair(k_ref[here, cols], masks),
                TN, preferred_element_type=jnp.float32,
            ) * inv_root).astype(jnp.bfloat16)
            left_ref[1, here, cols] = (jnp.dot(
                jnp.concatenate(score_wide, axis=1), split_pair(q_ref[here, cols], masks),
                preferred_element_type=jnp.float32,
            ) * inv_root).astype(jnp.bfloat16)
            left_ref[2, here, cols] = jnp.dot(
                jnp.concatenate(prob_wide, axis=1), split_pair(g_pair, masks),
                preferred_element_type=jnp.float32,
            ).astype(jnp.bfloat16)

    order = reorder_matrix(frames, toks, False)
    for col in range(0, channels, BLOCK):
        cols = slice(col, col + BLOCK)
        total = sum(
            lax.dot_general(left_ref[index], weight_ref[cols, :], NT, preferred_element_type=jnp.float32)
            for index, weight_ref in enumerate((wq_ref, wk_ref, wv_ref))
        )
        source = jnp.dot(order, total.astype(jnp.bfloat16), preferred_element_type=jnp.float32)
        result_ref[:, cols] = (
            source
            + taps_ref[0:1, cols] * pltpu.roll(source, rows - toks, 0)
            + taps_ref[1:2, cols] * source
            + taps_ref[2:3, cols] * pltpu.roll(source, toks, 0)
        ).astype(jnp.bfloat16)
    for mask in range(peers):
        start = pl.multiple_of((me ^ mask) * part, part)
        outs[mask][...] = result_ref[pl.ds(start, part), :]


def swap(value, axis, mask):
    return lax.ppermute(value, axis, [(i, i ^ mask) for i in range(lax.axis_size(axis))])


def grant(mebibytes):
    return pltpu.CompilerParams(vmem_limit_bytes=mebibytes << 20)


def on_chip(value):
    return pltpu.with_memory_space_constraint(value, pltpu.VMEM)


def off_chip(value):
    return pltpu.with_memory_space_constraint(value, pltpu.HBM)


def far_first(peers):
    return sorted(range(1, peers), key=lambda mask: (-bin(mask >> 1).count("1"), -mask))


def gather_tokens(sent):
    peers = lax.axis_size("orbit")
    _, frame_rows, toks, channels = sent[0].shape
    parts = [sent[0]] + [None] * (peers // 2 - 1)
    for mask in far_first(peers):
        if mask % 2 == 0:
            parts[mask // 2] = swap(sent[mask // 2], "orbit", mask)
    blocks = []
    for chip in range(peers // 2):
        pair = parts[chip].reshape(2, frame_rows * toks, channels)
        mine = pair[1]
        blocks += [pair, swap(mine, "orbit", 1)]
    return blocks


def spread_frames(blocks):
    peers = len(blocks)
    received = [blocks[0]] + [None] * (peers - 1)
    for mask in far_first(peers):
        received[mask] = swap(blocks[mask], "orbit", mask)
    return received


def tile_terms(value):
    terms = [value]
    for stage in range(lax.axis_size("tile").bit_length() - 1):
        value = sum(terms[1:], terms[0])
        terms = [value, swap(value, "tile", 1 << stage)]
    return terms


def body(tokens, cotangent, w_query, w_key, w_value, conv_taps, conv_bias):
    frame_rows, tile_rows, channels = tokens.shape
    peers = lax.axis_size("orbit")
    me = lax.axis_index("orbit")
    frames = frame_rows * peers
    toks = tile_rows // peers
    rows = frames * toks
    part = frame_rows * toks
    spatial_all = tile_rows * lax.axis_size("tile")
    heads = channels // HEAD_DIM
    me_arg = me.astype(jnp.int32).reshape(1)
    smem = pl.BlockSpec(memory_space=pltpu.SMEM)
    vmem = pl.BlockSpec(memory_space=pltpu.VMEM)
    hbm = pl.BlockSpec(memory_space=pltpu.HBM)
    low = functools.partial(pltpu.VMEM, dtype=jnp.bfloat16)
    sent_shape = low((2, frame_rows, toks, channels))
    split = (frame_rows, peers, toks, channels)

    *sent_tokens, energy, held = pl.pallas_call(
        functools.partial(pack_kernel, peers=peers),
        in_specs=[smem, hbm, hbm],
        out_specs=[vmem] * (peers // 2 + 2),
        out_shape=[sent_shape] * (peers // 2)
        + [pltpu.VMEM((frame_rows, LANES), jnp.float32), low(split)],
        scratch_shapes=[pltpu.SemaphoreType.DMA((peers + frame_rows,))],
        compiler_params=grant(8),
        name="pack",
    )(me_arg, off_chip(tokens.reshape(split)), off_chip(cotangent.reshape(split)))
    token_blocks = gather_tokens(sent_tokens)
    terms = tile_terms(energy)
    sent_grads = pl.pallas_call(
        functools.partial(scale_kernel, peers=peers, count=spatial_all * channels),
        in_specs=[smem] + [vmem] * (1 + len(terms)),
        out_specs=[vmem] * (peers // 2),
        out_shape=[sent_shape] * (peers // 2),
        compiler_params=grant(8),
        cost_estimate=pl.CostEstimate(flops=1 << 34, bytes_accessed=1 << 25, transcendentals=0),
        name="scale",
    )(me_arg, on_chip(held), *map(on_chip, terms))
    grad_blocks = gather_tokens(sent_grads)

    weights = (w_query, w_key, w_value)
    sizes = dict(frames=frames, toks=toks, peers=peers)
    query, key, value, prob = pl.pallas_call(
        functools.partial(forward_kernel, **sizes),
        in_specs=[smem] + [vmem] * (5 + peers),
        out_specs=[vmem] * 4,
        out_shape=[low((rows, channels))] * 3 + [pltpu.VMEM((heads, frames, rows), jnp.float32)],
        scratch_shapes=[
            pltpu.VMEM((rows, channels), jnp.float32), pltpu.VMEM((rows, channels), jnp.bfloat16)
        ],
        compiler_params=grant(20),
        name="forward",
    )(me_arg, conv_taps, conv_bias, *weights, *map(on_chip, token_blocks))
    results = pl.pallas_call(
        functools.partial(backward_kernel, **sizes),
        in_specs=[smem] + [vmem] * (8 + peers),
        out_specs=[vmem] * peers,
        out_shape=[low((part, channels))] * peers,
        scratch_shapes=[
            pltpu.VMEM((rows, channels), jnp.bfloat16),
            pltpu.VMEM((3, rows, channels), jnp.bfloat16),
            pltpu.VMEM((rows, channels), jnp.bfloat16),
        ],
        compiler_params=grant(20),
        name="backward",
    )(me_arg, conv_taps, *weights, *map(on_chip, (query, key, value, prob)), *map(on_chip, grad_blocks))
    received = [block.reshape(frame_rows, toks, channels) for block in spread_frames(results)]
    output = pl.pallas_call(
        functools.partial(place_kernel, peers=peers),
        in_specs=[smem] + [vmem] * peers,
        out_specs=hbm,
        out_shape=jax.ShapeDtypeStruct(split, jnp.bfloat16),
        scratch_shapes=[pltpu.SemaphoreType.DMA((peers,))],
        compiler_params=grant(4),
        name="place",
    )(me_arg, *map(on_chip, received))
    return output.reshape(frame_rows, tile_rows, channels)


def solution(mesh):
    in_specs = (P("orbit", "tile", None), P("orbit", "tile", None), P(), P(), P(), P(), P())
    out_specs = P("orbit", "tile", None)
    return jax.shard_map(body, mesh=mesh, in_specs=in_specs, out_specs=out_specs, check_vma=False)
```

```python
import functools
import math

import jax
import jax.numpy as jnp
from jax import lax
from jax.experimental import pallas as pl
from jax.experimental.pallas import tpu as pltpu
from jax.sharding import PartitionSpec as P


HEAD_DIM = 64
LANES = 128
BLOCK = 256
NT = (((1,), (1,)), ((), ()))
TN = (((0,), (0,)), ((), ()))


def iota(shape, dim):
    return lax.broadcasted_iota(jnp.int32, shape, dim)


def reorder_matrix(frames, toks, to_token_major):
    rows = frames * toks
    out_row = iota((rows, rows), 0)
    in_row = iota((rows, rows), 1)
    if to_token_major:
        source = (out_row % frames) * toks + out_row // frames
    else:
        source = (out_row % toks) * frames + out_row // toks
    return (in_row == source).astype(jnp.float32).astype(jnp.bfloat16)


def half_masks(rows):
    low = (iota((rows, LANES), 1) < HEAD_DIM).astype(jnp.float32)
    return low.astype(jnp.bfloat16), (1.0 - low).astype(jnp.bfloat16)


def split_pair(block, masks):
    return jnp.concatenate([block * masks[0], block * masks[1]], axis=0)


def compact(full, frames):
    token_of = iota((frames, LANES), 1) // frames
    kept = full[:frames]
    for tok in range(1, LANES // frames):
        kept = jnp.where(token_of == tok, full[tok * frames:(tok + 1) * frames], kept)
    return kept


def expand(kept, token_masks):
    return jnp.concatenate([kept * mask for mask in token_masks], axis=0)


def pack_kernel(me_ref, tokens_ref, cotangent_ref, *refs, peers):
    outs = refs[:peers // 2]
    energy_ref, held_ref, sems = refs[peers // 2:]
    me = me_ref[0]
    frame_rows = held_ref.shape[0]
    frame_copies = [
        pltpu.make_async_copy(cotangent_ref.at[frame], held_ref.at[frame], sems.at[peers + frame])
        for frame in range(frame_rows)
    ]
    copies = [
        pltpu.make_async_copy(
            tokens_ref.at[:, me ^ mask], outs[mask // 2].at[mask % 2], sems.at[mask]
        )
        for mask in range(peers)
    ]
    for copy in frame_copies + copies:
        copy.start()
    for frame in range(frame_rows):
        frame_copies[frame].wait()
        total = jnp.zeros(held_ref.shape[2:], jnp.float32)
        for group in range(peers):
            grad = held_ref[frame, group].astype(jnp.float32)
            total += grad * grad
        energy_ref[frame:frame + 1, :] = jnp.broadcast_to(
            jnp.sum(total, keepdims=True), (1, LANES)
        )
    for copy in copies:
        copy.wait()


def scale_kernel(me_ref, held_ref, *refs, peers, count):
    energies, outs = refs[:-(peers // 2)], refs[-(peers // 2):]
    me = me_ref[0]
    factor = lax.rsqrt(sum(energy[...] for energy in energies) / count + 1e-06)
    frame_rows = held_ref.shape[0]
    for mask in range(peers):
        for frame in range(frame_rows):
            grad = held_ref[frame, me ^ mask].astype(jnp.float32)
            outs[mask // 2][mask % 2, frame] = (
                grad * factor[frame:frame + 1, :1]
            ).astype(jnp.bfloat16)


def place_kernel(me_ref, *refs, peers):
    blocks = refs[:peers]
    out_ref, sems = refs[peers:]
    me = me_ref[0]
    copies = [
        pltpu.make_async_copy(blocks[mask], out_ref.at[:, me ^ mask], sems.at[mask])
        for mask in range(peers)
    ]
    for copy in copies:
        copy.start()
    for copy in copies:
        copy.wait()


def block_of(blocks, mask):
    block = blocks[mask][...]
    return block[0] if mask % 2 == 0 else block


def order_kernel(order_ref, *, frames, toks):
    order_ref[0] = reorder_matrix(frames, toks, True)
    order_ref[1] = reorder_matrix(frames, toks, False)


def forward_kernel(me_ref, order_ref, taps_ref, bias_ref, wq_ref, wk_ref, wv_ref, *refs,
                   frames, toks, peers):
    blocks = refs[:peers]
    q_ref, k_ref, v_ref, prob_ref, source_ref, hidden_ref = refs[peers:]
    rows, channels = hidden_ref.shape
    part = rows // peers
    me = me_ref[0]
    for mask in range(peers):
        start = pl.multiple_of((me ^ mask) * part, part)
        source_ref[pl.ds(start, part), :] = block_of(blocks, mask).astype(jnp.float32)
    for col in range(0, channels, BLOCK):
        cols = slice(col, col + BLOCK)
        source = source_ref[:, cols]
        mixed = (
            taps_ref[0:1, cols] * pltpu.roll(source, toks, 0)
            + taps_ref[1:2, cols] * source
            + taps_ref[2:3, cols] * pltpu.roll(source, rows - toks, 0)
        )
        hidden = (source + mixed + bias_ref[cols].reshape(1, BLOCK)).astype(jnp.bfloat16)
        hidden_ref[:, cols] = jnp.dot(
            order_ref[0], hidden, preferred_element_type=jnp.float32
        ).astype(jnp.bfloat16)

    masks = half_masks(LANES)
    inv_root = 1.0 / math.sqrt(HEAD_DIM)
    for col in range(0, channels, BLOCK):
        block = slice(col, col + BLOCK)
        for weight_ref, out_ref in ((wq_ref, q_ref), (wk_ref, k_ref), (wv_ref, v_ref)):
            out_ref[:, block] = jnp.dot(
                hidden_ref[...], weight_ref[:, block], preferred_element_type=jnp.float32
            ).astype(jnp.bfloat16)
        for start in range(col, col + BLOCK, LANES):
            cols = slice(start, start + LANES)
            for row in range(0, rows, LANES):
                here = slice(row, row + LANES)
                full = lax.dot_general(
                    split_pair(k_ref[here, cols], masks), q_ref[here, cols],
                    NT, preferred_element_type=jnp.float32,
                )
                for head in range(2):
                    scores = compact(full[head * LANES:(head + 1) * LANES], frames) * inv_root
                    expo = jnp.exp(scores - jnp.max(scores, axis=0, keepdims=True))
                    inverse = 1.0 / jnp.sum(expo, axis=0, keepdims=True)
                    prob_ref[start // HEAD_DIM + head, :, here] = expo * inverse


def backward_kernel(me_ref, order_ref, taps_ref, wq_ref, wk_ref, wv_ref, q_ref, k_ref, v_ref,
                    prob_ref, *refs, frames, toks, peers):
    blocks = refs[:peers]
    outs = refs[peers:2 * peers]
    grad_ref, left_ref, result_ref = refs[2 * peers:]
    rows, channels = grad_ref.shape
    part = rows // peers
    me = me_ref[0]
    for mask in range(peers):
        start = pl.multiple_of((me ^ mask) * part, part)
        result_ref[pl.ds(start, part), :] = block_of(blocks, mask)
    for col in range(0, channels, BLOCK):
        cols = slice(col, col + BLOCK)
        grad_ref[:, cols] = jnp.dot(
            order_ref[0], result_ref[:, cols], preferred_element_type=jnp.float32
        ).astype(jnp.bfloat16)

    masks = half_masks(LANES)
    token_of = iota((frames, LANES), 1) // frames
    token_masks = [
        (token_of == tok).astype(jnp.float32).astype(jnp.bfloat16) for tok in range(LANES // frames)
    ]
    inv_root = 1.0 / math.sqrt(HEAD_DIM)
    places = [
        (slice(row, row + LANES), slice(col, col + LANES), col // HEAD_DIM)
        for col in range(0, channels, LANES) for row in range(0, rows, LANES)
    ]

    def grad_probs(here, cols, head):
        return lax.dot_general(
            split_pair(v_ref[here, cols], masks), grad_ref[here, cols],
            NT, preferred_element_type=jnp.float32,
        )

    def widen(full, here, cols, head):
        prob_wide, score_wide = [], []
        for half in range(2):
            prob = prob_ref[head + half, :, here]
            prob_low = prob.astype(jnp.bfloat16)
            grad_prob = compact(full[half * LANES:(half + 1) * LANES], frames)
            delta = jnp.sum(prob_low.astype(jnp.float32) * grad_prob, axis=0, keepdims=True)
            d_scores = (prob * (grad_prob - delta)).astype(jnp.bfloat16)
            prob_wide.append(expand(prob_low, token_masks))
            score_wide.append(expand(d_scores, token_masks))
        return prob_wide, score_wide

    def contract(wide, here, cols, head):
        prob_wide, score_wide = wide
        left_ref[0, here, cols] = (lax.dot_general(
            jnp.concatenate(score_wide, axis=0), split_pair(k_ref[here, cols], masks),
            TN, preferred_element_type=jnp.float32,
        ) * inv_root).astype(jnp.bfloat16)
        left_ref[1, here, cols] = (jnp.dot(
            jnp.concatenate(score_wide, axis=1), split_pair(q_ref[here, cols], masks),
            preferred_element_type=jnp.float32,
        ) * inv_root).astype(jnp.bfloat16)
        left_ref[2, here, cols] = jnp.dot(
            jnp.concatenate(prob_wide, axis=1), split_pair(grad_ref[here, cols], masks),
            preferred_element_type=jnp.float32,
        ).astype(jnp.bfloat16)

    fulls, wides = {}, {}
    for index in range(len(places) + 2):
        if index < len(places):
            fulls[index] = grad_probs(*places[index])
        if 0 <= index - 1 < len(places):
            wides[index - 1] = widen(fulls.pop(index - 1), *places[index - 1])
        if 0 <= index - 2:
            contract(wides.pop(index - 2), *places[index - 2])

    total = sum(
        lax.dot_general(weight_ref[...], left_ref[index], NT, preferred_element_type=jnp.float32)
        for index, weight_ref in enumerate((wq_ref, wk_ref, wv_ref))
    ).astype(jnp.bfloat16)
    for col in range(0, channels, BLOCK):
        cols = slice(col, col + BLOCK)
        source = lax.dot_general(
            order_ref[1], total[cols], NT, preferred_element_type=jnp.float32
        )
        result_ref[:, cols] = (
            source
            + taps_ref[0:1, cols] * pltpu.roll(source, rows - toks, 0)
            + taps_ref[1:2, cols] * source
            + taps_ref[2:3, cols] * pltpu.roll(source, toks, 0)
        ).astype(jnp.bfloat16)
    for mask in range(peers):
        start = pl.multiple_of((me ^ mask) * part, part)
        outs[mask][...] = result_ref[pl.ds(start, part), :]


def swap(value, axis, mask):
    return lax.ppermute(value, axis, [(i, i ^ mask) for i in range(lax.axis_size(axis))])


def grant(mebibytes):
    return pltpu.CompilerParams(vmem_limit_bytes=mebibytes << 20)


def on_chip(value):
    return pltpu.with_memory_space_constraint(value, pltpu.VMEM)


def off_chip(value):
    return pltpu.with_memory_space_constraint(value, pltpu.HBM)


def far_first(peers):
    return sorted(range(1, peers), key=lambda mask: (-bin(mask >> 1).count("1"), -mask))


def gather_tokens(sent):
    peers = lax.axis_size("orbit")
    _, frame_rows, toks, channels = sent[0].shape
    parts = [sent[0]] + [None] * (peers // 2 - 1)
    for mask in far_first(peers):
        if mask % 2 == 0:
            parts[mask // 2] = swap(sent[mask // 2], "orbit", mask)
    blocks = []
    for chip in range(peers // 2):
        pair = parts[chip].reshape(2, frame_rows * toks, channels)
        mine = pair[1]
        blocks += [pair, swap(mine, "orbit", 1)]
    return blocks


def spread_frames(blocks):
    peers = len(blocks)
    received = [blocks[0]] + [None] * (peers - 1)
    for mask in far_first(peers):
        received[mask] = swap(blocks[mask], "orbit", mask)
    return received


def tile_terms(value):
    terms = [value]
    for stage in range(lax.axis_size("tile").bit_length() - 1):
        value = sum(terms[1:], terms[0])
        terms = [value, swap(value, "tile", 1 << stage)]
    return terms


def body(tokens, cotangent, w_query, w_key, w_value, conv_taps, conv_bias):
    frame_rows, tile_rows, channels = tokens.shape
    peers = lax.axis_size("orbit")
    me = lax.axis_index("orbit")
    frames = frame_rows * peers
    toks = tile_rows // peers
    rows = frames * toks
    part = frame_rows * toks
    spatial_all = tile_rows * lax.axis_size("tile")
    heads = channels // HEAD_DIM
    me_arg = me.astype(jnp.int32).reshape(1)
    smem = pl.BlockSpec(memory_space=pltpu.SMEM)
    vmem = pl.BlockSpec(memory_space=pltpu.VMEM)
    hbm = pl.BlockSpec(memory_space=pltpu.HBM)
    low = functools.partial(pltpu.VMEM, dtype=jnp.bfloat16)
    sent_shape = low((2, frame_rows, toks, channels))
    split = (frame_rows, peers, toks, channels)

    *sent_tokens, energy, held = pl.pallas_call(
        functools.partial(pack_kernel, peers=peers),
        in_specs=[smem, hbm, hbm],
        out_specs=[vmem] * (peers // 2 + 2),
        out_shape=[sent_shape] * (peers // 2)
        + [pltpu.VMEM((frame_rows, LANES), jnp.float32), low(split)],
        scratch_shapes=[pltpu.SemaphoreType.DMA((peers + frame_rows,))],
        compiler_params=grant(8),
        name="pack",
    )(me_arg, off_chip(tokens.reshape(split)), off_chip(cotangent.reshape(split)))
    token_blocks = gather_tokens(sent_tokens)
    terms = tile_terms(energy)
    sent_grads = pl.pallas_call(
        functools.partial(scale_kernel, peers=peers, count=spatial_all * channels),
        in_specs=[smem] + [vmem] * (1 + len(terms)),
        out_specs=[vmem] * (peers // 2),
        out_shape=[sent_shape] * (peers // 2),
        compiler_params=grant(8),
        cost_estimate=pl.CostEstimate(flops=1 << 34, bytes_accessed=1 << 25, transcendentals=0),
        name="scale",
    )(me_arg, on_chip(held), *map(on_chip, terms))
    grad_blocks = gather_tokens(sent_grads)

    weights = (w_query, w_key, w_value)
    sizes = dict(frames=frames, toks=toks, peers=peers)
    order = on_chip(pl.pallas_call(
        functools.partial(order_kernel, frames=frames, toks=toks),
        out_specs=vmem,
        out_shape=low((2, rows, rows)),
        compiler_params=grant(4),
        name="order",
    )())
    query, key, value, prob = pl.pallas_call(
        functools.partial(forward_kernel, **sizes),
        in_specs=[smem] + [vmem] * (6 + peers),
        out_specs=[vmem] * 4,
        out_shape=[low((rows, channels))] * 3 + [pltpu.VMEM((heads, frames, rows), jnp.float32)],
        scratch_shapes=[
            pltpu.VMEM((rows, channels), jnp.float32), pltpu.VMEM((rows, channels), jnp.bfloat16)
        ],
        compiler_params=grant(20),
        name="forward",
    )(me_arg, order, conv_taps, conv_bias, *weights, *map(on_chip, token_blocks))
    results = pl.pallas_call(
        functools.partial(backward_kernel, **sizes),
        in_specs=[smem] + [vmem] * (9 + peers),
        out_specs=[vmem] * peers,
        out_shape=[low((part, channels))] * peers,
        scratch_shapes=[
            pltpu.VMEM((rows, channels), jnp.bfloat16),
            pltpu.VMEM((3, rows, channels), jnp.bfloat16),
            pltpu.VMEM((rows, channels), jnp.bfloat16),
        ],
        compiler_params=grant(20),
        name="backward",
    )(me_arg, order, conv_taps, *weights, *map(on_chip, (query, key, value, prob)), *map(on_chip, grad_blocks))
    received = [block.reshape(frame_rows, toks, channels) for block in spread_frames(results)]
    output = pl.pallas_call(
        functools.partial(place_kernel, peers=peers),
        in_specs=[smem] + [vmem] * peers,
        out_specs=hbm,
        out_shape=jax.ShapeDtypeStruct(split, jnp.bfloat16),
        scratch_shapes=[pltpu.SemaphoreType.DMA((peers,))],
        compiler_params=grant(4),
        name="place",
    )(me_arg, *map(on_chip, received))
    return output.reshape(frame_rows, tile_rows, channels)


def solution(mesh):
    in_specs = (P("orbit", "tile", None), P("orbit", "tile", None), P(), P(), P(), P(), P())
    out_specs = P("orbit", "tile", None)
    return jax.shard_map(body, mesh=mesh, in_specs=in_specs, out_specs=out_specs, check_vma=False)
```

```python
import functools
import math

import jax
import jax.numpy as jnp
from jax import lax
from jax.experimental import pallas as pl
from jax.experimental.pallas import tpu as pltpu
from jax.sharding import PartitionSpec as P


HEAD_DIM = 64
LANES = 128
BLOCK = 256
NT = (((1,), (1,)), ((), ()))
TN = (((0,), (0,)), ((), ()))


def iota(shape, dim):
    return lax.broadcasted_iota(jnp.int32, shape, dim)


def reorder_matrix(frames, toks, to_token_major):
    rows = frames * toks
    out_row = iota((rows, rows), 0)
    in_row = iota((rows, rows), 1)
    if to_token_major:
        source = (out_row % frames) * toks + out_row // frames
    else:
        source = (out_row % toks) * frames + out_row // toks
    return (in_row == source).astype(jnp.float32).astype(jnp.bfloat16)


def half_masks(rows):
    low = (iota((rows, LANES), 1) < HEAD_DIM).astype(jnp.float32)
    return low.astype(jnp.bfloat16), (1.0 - low).astype(jnp.bfloat16)


def split_pair(block, masks):
    return jnp.concatenate([block * masks[0], block * masks[1]], axis=0)


def compact(full, frames):
    token_of = iota((frames, LANES), 1) // frames
    kept = full[:frames]
    for tok in range(1, LANES // frames):
        kept = jnp.where(token_of == tok, full[tok * frames:(tok + 1) * frames], kept)
    return kept


def expand(kept, token_masks):
    return jnp.concatenate([kept * mask for mask in token_masks], axis=0)


def pack_kernel(me_ref, tokens_ref, cotangent_ref, *refs, peers):
    outs = refs[:peers // 2]
    energy_ref, held_ref, sems = refs[peers // 2:]
    me = me_ref[0]
    frame_rows = held_ref.shape[0]
    frame_copies = [
        pltpu.make_async_copy(cotangent_ref.at[frame], held_ref.at[frame], sems.at[peers + frame])
        for frame in range(frame_rows)
    ]
    copies = [
        pltpu.make_async_copy(
            tokens_ref.at[:, me ^ mask], outs[mask // 2].at[mask % 2], sems.at[mask]
        )
        for mask in range(peers)
    ]
    for copy in frame_copies + copies:
        copy.start()
    for frame in range(frame_rows):
        frame_copies[frame].wait()
        total = jnp.zeros(held_ref.shape[2:], jnp.float32)
        for group in range(peers):
            grad = held_ref[frame, group].astype(jnp.float32)
            total += grad * grad
        energy_ref[frame:frame + 1, :] = jnp.broadcast_to(
            jnp.sum(total, keepdims=True), (1, LANES)
        )
    for copy in copies:
        copy.wait()


def scale_kernel(me_ref, held_ref, *refs, peers, count):
    energies, outs = refs[:-(peers // 2)], refs[-(peers // 2):]
    me = me_ref[0]
    factor = lax.rsqrt(sum(energy[...] for energy in energies) / count + 1e-06)
    frame_rows = held_ref.shape[0]
    for mask in range(peers):
        for frame in range(frame_rows):
            grad = held_ref[frame, me ^ mask].astype(jnp.float32)
            outs[mask // 2][mask % 2, frame] = (
                grad * factor[frame:frame + 1, :1]
            ).astype(jnp.bfloat16)


def place_kernel(me_ref, *refs, masks):
    out_ref, sems = refs[-2:]
    me = me_ref[0]
    copies = [
        pltpu.make_async_copy(refs[index], out_ref.at[:, me ^ mask], sems.at[index])
        for index, mask in enumerate(masks)
    ]
    for copy in copies:
        copy.start()
    for copy in copies:
        copy.wait()


def join_kernel(*refs):
    for index, pair_ref in enumerate(refs[:-1]):
        refs[-1][index] = pair_ref[1]


def block_of(blocks, mask):
    chip = mask // 2
    if mask % 2 == 0:
        return blocks[chip][0]
    return blocks[-1][chip - 1] if chip else blocks[-2][...]


def order_kernel(order_ref, *, frames, toks):
    order_ref[0] = reorder_matrix(frames, toks, True)
    order_ref[1] = reorder_matrix(frames, toks, False)


def forward_kernel(me_ref, order_ref, taps_ref, bias_ref, wq_ref, wk_ref, wv_ref, *refs,
                   frames, toks, peers):
    blocks = refs[:peers // 2 + 2]
    q_ref, k_ref, v_ref, prob_ref, source_ref, hidden_ref = refs[peers // 2 + 2:]
    rows, channels = hidden_ref.shape
    part = rows // peers
    me = me_ref[0]
    for mask in range(peers):
        start = pl.multiple_of((me ^ mask) * part, part)
        source_ref[pl.ds(start, part), :] = block_of(blocks, mask).astype(jnp.float32)
    for col in range(0, channels, BLOCK):
        cols = slice(col, col + BLOCK)
        source = source_ref[:, cols]
        mixed = (
            taps_ref[0:1, cols] * pltpu.roll(source, toks, 0)
            + taps_ref[1:2, cols] * source
            + taps_ref[2:3, cols] * pltpu.roll(source, rows - toks, 0)
        )
        hidden = (source + mixed + bias_ref[cols].reshape(1, BLOCK)).astype(jnp.bfloat16)
        hidden_ref[:, cols] = jnp.dot(
            order_ref[0], hidden, preferred_element_type=jnp.float32
        ).astype(jnp.bfloat16)

    masks = half_masks(LANES)
    inv_root = 1.0 / math.sqrt(HEAD_DIM)
    for col in range(0, channels, BLOCK):
        block = slice(col, col + BLOCK)
        for weight_ref, out_ref in ((wq_ref, q_ref), (wk_ref, k_ref), (wv_ref, v_ref)):
            out_ref[:, block] = jnp.dot(
                hidden_ref[...], weight_ref[:, block], preferred_element_type=jnp.float32
            ).astype(jnp.bfloat16)
        for start in range(col, col + BLOCK, LANES):
            cols = slice(start, start + LANES)
            for row in range(0, rows, LANES):
                here = slice(row, row + LANES)
                full = lax.dot_general(
                    split_pair(k_ref[here, cols], masks), q_ref[here, cols],
                    NT, preferred_element_type=jnp.float32,
                )
                for head in range(2):
                    scores = compact(full[head * LANES:(head + 1) * LANES], frames) * inv_root
                    expo = jnp.exp(scores - jnp.max(scores, axis=0, keepdims=True))
                    inverse = 1.0 / jnp.sum(expo, axis=0, keepdims=True)
                    prob_ref[start // HEAD_DIM + head, :, here] = expo * inverse


def backward_kernel(me_ref, order_ref, taps_ref, wq_ref, wk_ref, wv_ref, q_ref, k_ref, v_ref,
                    prob_ref, *refs, frames, toks, peers):
    blocks = refs[:peers // 2 + 2]
    outs = refs[peers // 2 + 2:-3]
    grad_ref, left_ref, result_ref = refs[-3:]
    rows, channels = grad_ref.shape
    part = rows // peers
    me = me_ref[0]
    for mask in range(peers):
        start = pl.multiple_of((me ^ mask) * part, part)
        result_ref[pl.ds(start, part), :] = block_of(blocks, mask)
    for col in range(0, channels, BLOCK):
        cols = slice(col, col + BLOCK)
        grad_ref[:, cols] = jnp.dot(
            order_ref[0], result_ref[:, cols], preferred_element_type=jnp.float32
        ).astype(jnp.bfloat16)

    masks = half_masks(LANES)
    token_of = iota((frames, LANES), 1) // frames
    token_masks = [
        (token_of == tok).astype(jnp.float32).astype(jnp.bfloat16) for tok in range(LANES // frames)
    ]
    inv_root = 1.0 / math.sqrt(HEAD_DIM)
    places = [
        (slice(row, row + LANES), slice(col, col + LANES), col // HEAD_DIM)
        for col in range(0, channels, LANES) for row in range(0, rows, LANES)
    ]

    def grad_probs(here, cols, head):
        return lax.dot_general(
            split_pair(v_ref[here, cols], masks), grad_ref[here, cols],
            NT, preferred_element_type=jnp.float32,
        )

    def widen(full, here, cols, head):
        prob_wide, score_wide = [], []
        for half in range(2):
            prob = prob_ref[head + half, :, here]
            prob_low = prob.astype(jnp.bfloat16)
            grad_prob = compact(full[half * LANES:(half + 1) * LANES], frames)
            delta = jnp.sum(prob_low.astype(jnp.float32) * grad_prob, axis=0, keepdims=True)
            d_scores = (prob * (grad_prob - delta)).astype(jnp.bfloat16)
            prob_wide.append(expand(prob_low, token_masks))
            score_wide.append(expand(d_scores, token_masks))
        return prob_wide, score_wide

    def contract(wide, here, cols, head):
        prob_wide, score_wide = wide
        left_ref[0, here, cols] = (lax.dot_general(
            jnp.concatenate(score_wide, axis=0), split_pair(k_ref[here, cols], masks),
            TN, preferred_element_type=jnp.float32,
        ) * inv_root).astype(jnp.bfloat16)
        left_ref[1, here, cols] = (jnp.dot(
            jnp.concatenate(score_wide, axis=1), split_pair(q_ref[here, cols], masks),
            preferred_element_type=jnp.float32,
        ) * inv_root).astype(jnp.bfloat16)
        left_ref[2, here, cols] = jnp.dot(
            jnp.concatenate(prob_wide, axis=1), split_pair(grad_ref[here, cols], masks),
            preferred_element_type=jnp.float32,
        ).astype(jnp.bfloat16)

    fulls, wides = {}, {}
    for index in range(len(places) + 2):
        if index < len(places):
            fulls[index] = grad_probs(*places[index])
        if 0 <= index - 1 < len(places):
            wides[index - 1] = widen(fulls.pop(index - 1), *places[index - 1])
        if 0 <= index - 2:
            contract(wides.pop(index - 2), *places[index - 2])

    total = sum(
        lax.dot_general(weight_ref[...], left_ref[index], NT, preferred_element_type=jnp.float32)
        for index, weight_ref in enumerate((wq_ref, wk_ref, wv_ref))
    ).astype(jnp.bfloat16)
    for col in range(0, channels, BLOCK):
        cols = slice(col, col + BLOCK)
        source = lax.dot_general(
            order_ref[1], total[cols], NT, preferred_element_type=jnp.float32
        )
        result_ref[:, cols] = (
            source
            + taps_ref[0:1, cols] * pltpu.roll(source, rows - toks, 0)
            + taps_ref[1:2, cols] * source
            + taps_ref[2:3, cols] * pltpu.roll(source, toks, 0)
        ).astype(jnp.bfloat16)
    for mask in range(peers):
        start = pl.multiple_of((me ^ mask) * part, part)
        outs[mask][...] = result_ref[pl.ds(start, part), :]


def swap(value, axis, mask):
    return lax.ppermute(value, axis, [(i, i ^ mask) for i in range(lax.axis_size(axis))])


def grant(mebibytes):
    return pltpu.CompilerParams(vmem_limit_bytes=mebibytes << 20)


def on_chip(value):
    return pltpu.with_memory_space_constraint(value, pltpu.VMEM)


def off_chip(value):
    return pltpu.with_memory_space_constraint(value, pltpu.HBM)


def far_first(peers):
    masks = sorted(range(2, peers), key=lambda mask: (-bin(mask >> 1).count("1"), mask & 1, -mask))
    return masks + [1]


def gather_tokens(sent):
    peers = lax.axis_size("orbit")
    _, frame_rows, toks, channels = sent[0].shape
    parts = [sent[0]] + [None] * (peers // 2 - 1)
    for mask in far_first(peers):
        if mask % 2 == 0:
            parts[mask // 2] = swap(sent[mask // 2], "orbit", mask)
    parts = [part.reshape(2, frame_rows * toks, channels) for part in parts]
    own = swap(parts[0][1], "orbit", 1)
    others = pl.pallas_call(
        join_kernel,
        in_specs=[pl.BlockSpec(memory_space=pltpu.VMEM)] * (peers // 2 - 1),
        out_specs=pl.BlockSpec(memory_space=pltpu.VMEM),
        out_shape=pltpu.VMEM((peers // 2 - 1, frame_rows * toks, channels), jnp.bfloat16),
        compiler_params=grant(4),
        name="join",
    )(*map(on_chip, parts[1:]))
    return parts + [own, swap(others, "orbit", 1)]


def spread_frames(blocks):
    peers = len(blocks)
    received = [blocks[0]] + [None] * (peers - 1)
    for mask in far_first(peers):
        received[mask] = swap(blocks[mask], "orbit", mask)
    return received


def tile_terms(value):
    terms = [value]
    for stage in range(lax.axis_size("tile").bit_length() - 1):
        value = sum(terms[1:], terms[0])
        terms = [value, swap(value, "tile", 1 << stage)]
    return terms


def body(tokens, cotangent, w_query, w_key, w_value, conv_taps, conv_bias):
    frame_rows, tile_rows, channels = tokens.shape
    peers = lax.axis_size("orbit")
    me = lax.axis_index("orbit")
    frames = frame_rows * peers
    toks = tile_rows // peers
    rows = frames * toks
    part = frame_rows * toks
    spatial_all = tile_rows * lax.axis_size("tile")
    heads = channels // HEAD_DIM
    me_arg = me.astype(jnp.int32).reshape(1)
    smem = pl.BlockSpec(memory_space=pltpu.SMEM)
    vmem = pl.BlockSpec(memory_space=pltpu.VMEM)
    hbm = pl.BlockSpec(memory_space=pltpu.HBM)
    low = functools.partial(pltpu.VMEM, dtype=jnp.bfloat16)
    sent_shape = low((2, frame_rows, toks, channels))
    split = (frame_rows, peers, toks, channels)

    *sent_tokens, energy, held = pl.pallas_call(
        functools.partial(pack_kernel, peers=peers),
        in_specs=[smem, hbm, hbm],
        out_specs=[vmem] * (peers // 2 + 2),
        out_shape=[sent_shape] * (peers // 2)
        + [pltpu.VMEM((frame_rows, LANES), jnp.float32), low(split)],
        scratch_shapes=[pltpu.SemaphoreType.DMA((peers + frame_rows,))],
        compiler_params=grant(8),
        name="pack",
    )(me_arg, off_chip(tokens.reshape(split)), off_chip(cotangent.reshape(split)))
    token_blocks = gather_tokens(sent_tokens)
    terms = tile_terms(energy)
    sent_grads = pl.pallas_call(
        functools.partial(scale_kernel, peers=peers, count=spatial_all * channels),
        in_specs=[smem] + [vmem] * (1 + len(terms)),
        out_specs=[vmem] * (peers // 2),
        out_shape=[sent_shape] * (peers // 2),
        compiler_params=grant(8),
        cost_estimate=pl.CostEstimate(flops=1 << 34, bytes_accessed=1 << 25, transcendentals=0),
        name="scale",
    )(me_arg, on_chip(held), *map(on_chip, terms))
    grad_blocks = gather_tokens(sent_grads)

    weights = (w_query, w_key, w_value)
    sizes = dict(frames=frames, toks=toks, peers=peers)
    order = on_chip(pl.pallas_call(
        functools.partial(order_kernel, frames=frames, toks=toks),
        out_specs=vmem,
        out_shape=low((2, rows, rows)),
        compiler_params=grant(4),
        name="order",
    )())
    query, key, value, prob = pl.pallas_call(
        functools.partial(forward_kernel, **sizes),
        in_specs=[smem] + [vmem] * (8 + peers // 2),
        out_specs=[vmem] * 4,
        out_shape=[low((rows, channels))] * 3 + [pltpu.VMEM((heads, frames, rows), jnp.float32)],
        scratch_shapes=[
            pltpu.VMEM((rows, channels), jnp.float32), pltpu.VMEM((rows, channels), jnp.bfloat16)
        ],
        compiler_params=grant(20),
        name="forward",
    )(me_arg, order, conv_taps, conv_bias, *weights, *map(on_chip, token_blocks))
    results = pl.pallas_call(
        functools.partial(backward_kernel, **sizes),
        in_specs=[smem] + [vmem] * (11 + peers // 2),
        out_specs=[vmem] * peers,
        out_shape=[low((part, channels))] * peers,
        scratch_shapes=[
            pltpu.VMEM((rows, channels), jnp.bfloat16),
            pltpu.VMEM((3, rows, channels), jnp.bfloat16),
            pltpu.VMEM((rows, channels), jnp.bfloat16),
        ],
        compiler_params=grant(20),
        name="backward",
    )(me_arg, order, conv_taps, *weights, *map(on_chip, (query, key, value, prob)), *map(on_chip, grad_blocks))
    received = [block.reshape(frame_rows, toks, channels) for block in spread_frames(results)]
    early = [mask for mask in range(peers) if bin(mask >> 1).count("1") != 1]
    late = [mask for mask in range(peers) if mask not in early]
    output = None
    for masks in (early, late):
        blocks = [on_chip(received[mask]) for mask in masks]
        output = pl.pallas_call(
            functools.partial(place_kernel, masks=masks),
            in_specs=[smem] + [vmem] * len(masks) + [hbm] * (output is not None),
            out_specs=hbm,
            out_shape=jax.ShapeDtypeStruct(split, jnp.bfloat16),
            scratch_shapes=[pltpu.SemaphoreType.DMA((len(masks),))],
            input_output_aliases={} if output is None else {len(masks) + 1: 0},
            compiler_params=grant(4),
            name="place",
        )(me_arg, *blocks, *([] if output is None else [output]))
    return output.reshape(frame_rows, tile_rows, channels)


def solution(mesh):
    in_specs = (P("orbit", "tile", None), P("orbit", "tile", None), P(), P(), P(), P(), P())
    out_specs = P("orbit", "tile", None)
    return jax.shard_map(body, mesh=mesh, in_specs=in_specs, out_specs=out_specs, check_vma=False)
```

```python
import functools
import math

import jax
import jax.numpy as jnp
from jax import lax
from jax.experimental import pallas as pl
from jax.experimental.pallas import tpu as pltpu
from jax.sharding import PartitionSpec as P


HEAD_DIM = 64
LANES = 128
BLOCK = 256
NT = (((1,), (1,)), ((), ()))
TN = (((0,), (0,)), ((), ()))


def iota(shape, dim):
    return lax.broadcasted_iota(jnp.int32, shape, dim)


def reorder_matrix(frames, toks, to_token_major):
    rows = frames * toks
    out_row = iota((rows, rows), 0)
    in_row = iota((rows, rows), 1)
    if to_token_major:
        source = (out_row % frames) * toks + out_row // frames
    else:
        source = (out_row % toks) * frames + out_row // toks
    return (in_row == source).astype(jnp.float32).astype(jnp.bfloat16)


def half_masks(rows):
    low = (iota((rows, LANES), 1) < HEAD_DIM).astype(jnp.float32)
    return low.astype(jnp.bfloat16), (1.0 - low).astype(jnp.bfloat16)


def split_pair(block, masks):
    return jnp.concatenate([block * masks[0], block * masks[1]], axis=0)


def compact(full, frames):
    token_of = iota((frames, LANES), 1) // frames
    kept = full[:frames]
    for tok in range(1, LANES // frames):
        kept = jnp.where(token_of == tok, full[tok * frames:(tok + 1) * frames], kept)
    return kept


def expand(kept, token_masks):
    return jnp.concatenate([kept * mask for mask in token_masks], axis=0)


def pack_kernel(me_ref, tokens_ref, cotangent_ref, *refs, peers):
    outs = refs[:peers // 2]
    energy_ref, held_ref, sems = refs[peers // 2:]
    me = me_ref[0]
    frame_rows = held_ref.shape[0]
    frame_copies = [
        pltpu.make_async_copy(cotangent_ref.at[frame], held_ref.at[frame], sems.at[peers + frame])
        for frame in range(frame_rows)
    ]
    copies = [
        pltpu.make_async_copy(
            tokens_ref.at[:, me ^ mask], outs[mask // 2].at[mask % 2], sems.at[mask]
        )
        for mask in range(peers)
    ]
    for copy in frame_copies + copies:
        copy.start()
    for frame in range(frame_rows):
        frame_copies[frame].wait()
        total = jnp.zeros(held_ref.shape[2:], jnp.float32)
        for group in range(peers):
            grad = held_ref[frame, group].astype(jnp.float32)
            total += grad * grad
        energy_ref[frame:frame + 1, :] = jnp.broadcast_to(
            jnp.sum(total, keepdims=True), (1, LANES)
        )
    for copy in copies:
        copy.wait()


def scale_kernel(me_ref, held_ref, *refs, peers, count):
    energies, outs = refs[:-(peers // 2)], refs[-(peers // 2):]
    me = me_ref[0]
    factor = lax.rsqrt(sum(energy[...] for energy in energies) / count + 1e-06)
    frame_rows = held_ref.shape[0]
    for mask in range(peers):
        for frame in range(frame_rows):
            grad = held_ref[frame, me ^ mask].astype(jnp.float32)
            outs[mask // 2][mask % 2, frame] = (
                grad * factor[frame:frame + 1, :1]
            ).astype(jnp.bfloat16)


def place_kernel(me_ref, *refs, masks):
    out_ref, sems = refs[-2:]
    me = me_ref[0]
    copies = [
        pltpu.make_async_copy(refs[index], out_ref.at[:, me ^ mask], sems.at[index])
        for index, mask in enumerate(masks)
    ]
    for copy in copies:
        copy.start()
    for copy in copies:
        copy.wait()


def join_kernel(*refs):
    for index, pair_ref in enumerate(refs[:-1]):
        refs[-1][index] = pair_ref[1]


def block_of(blocks, mask):
    chip = mask // 2
    if mask % 2 == 0:
        return blocks[chip][0]
    return blocks[-1][chip - 1] if chip else blocks[-2][...]


def order_kernel(order_ref, *, frames, toks):
    order_ref[0] = reorder_matrix(frames, toks, True)
    order_ref[1] = reorder_matrix(frames, toks, False)


def forward_kernel(me_ref, order_ref, taps_ref, bias_ref, wq_ref, wk_ref, *refs,
                   frames, toks, peers):
    blocks = refs[:peers // 2 + 2]
    q_ref, k_ref, prob_ref, hidden_ref, source_ref = refs[peers // 2 + 2:]
    rows, channels = hidden_ref.shape
    part = rows // peers
    me = me_ref[0]
    for mask in range(peers):
        start = pl.multiple_of((me ^ mask) * part, part)
        source_ref[pl.ds(start, part), :] = block_of(blocks, mask).astype(jnp.float32)
    for col in range(0, channels, BLOCK):
        cols = slice(col, col + BLOCK)
        source = source_ref[:, cols]
        hidden = (
            taps_ref[0:1, cols] * pltpu.roll(source, toks, 0)
            + (1.0 + taps_ref[1:2, cols]) * source
            + taps_ref[2:3, cols] * pltpu.roll(source, rows - toks, 0)
            + bias_ref[cols].reshape(1, BLOCK)
        ).astype(jnp.bfloat16)
        hidden_ref[:, cols] = jnp.dot(
            order_ref[0], hidden, preferred_element_type=jnp.float32
        ).astype(jnp.bfloat16)

    masks = half_masks(LANES)
    inv_root = 1.0 / math.sqrt(HEAD_DIM)
    for col in range(0, channels, BLOCK):
        block = slice(col, col + BLOCK)
        for weight_ref, out_ref in ((wq_ref, q_ref), (wk_ref, k_ref)):
            out_ref[:, block] = jnp.dot(
                hidden_ref[...], weight_ref[:, block], preferred_element_type=jnp.float32
            ).astype(jnp.bfloat16)
        for start in range(col, col + BLOCK, LANES):
            cols = slice(start, start + LANES)
            for row in range(0, rows, LANES):
                here = slice(row, row + LANES)
                full = lax.dot_general(
                    split_pair(k_ref[here, cols], masks), q_ref[here, cols],
                    NT, preferred_element_type=jnp.float32,
                )
                for head in range(2):
                    scores = compact(full[head * LANES:(head + 1) * LANES], frames) * inv_root
                    expo = jnp.exp(scores - jnp.max(scores, axis=0, keepdims=True))
                    inverse = 1.0 / jnp.sum(expo, axis=0, keepdims=True)
                    prob_ref[start // HEAD_DIM + head, :, here] = expo * inverse


def value_kernel(hidden_ref, wv_ref, v_ref):
    v_ref[...] = jnp.dot(
        hidden_ref[...], wv_ref[...], preferred_element_type=jnp.float32
    ).astype(jnp.bfloat16)


def backward_kernel(me_ref, order_ref, taps_ref, wq_ref, wk_ref, wv_ref, q_ref, k_ref, v_ref,
                    prob_ref, *refs, frames, toks, peers):
    blocks = refs[:peers // 2 + 2]
    outs = refs[peers // 2 + 2:-3]
    grad_ref, left_ref, result_ref = refs[-3:]
    rows, channels = grad_ref.shape
    part = rows // peers
    me = me_ref[0]
    for mask in range(peers):
        start = pl.multiple_of((me ^ mask) * part, part)
        result_ref[pl.ds(start, part), :] = block_of(blocks, mask)
    for col in range(0, channels, BLOCK):
        cols = slice(col, col + BLOCK)
        grad_ref[:, cols] = jnp.dot(
            order_ref[0], result_ref[:, cols], preferred_element_type=jnp.float32
        ).astype(jnp.bfloat16)

    masks = half_masks(LANES)
    token_of = iota((frames, LANES), 1) // frames
    token_masks = [
        (token_of == tok).astype(jnp.float32).astype(jnp.bfloat16) for tok in range(LANES // frames)
    ]
    inv_root = 1.0 / math.sqrt(HEAD_DIM)
    places = [
        (slice(row, row + LANES), slice(col, col + LANES), col // HEAD_DIM)
        for col in range(0, channels, LANES) for row in range(0, rows, LANES)
    ]

    def grad_probs(here, cols, head):
        return lax.dot_general(
            split_pair(v_ref[here, cols], masks), grad_ref[here, cols],
            NT, preferred_element_type=jnp.float32,
        )

    def widen(full, here, cols, head):
        prob_wide, score_wide = [], []
        for half in range(2):
            prob = prob_ref[head + half, :, here]
            prob_low = prob.astype(jnp.bfloat16)
            grad_prob = compact(full[half * LANES:(half + 1) * LANES], frames)
            delta = jnp.sum(prob_low.astype(jnp.float32) * grad_prob, axis=0, keepdims=True)
            d_scores = (prob * (grad_prob - delta)).astype(jnp.bfloat16)
            prob_wide.append(expand(prob_low, token_masks))
            score_wide.append(expand(d_scores, token_masks))
        return prob_wide, score_wide

    def contract(wide, here, cols, head):
        prob_wide, score_wide = wide
        left_ref[0, here, cols] = (lax.dot_general(
            jnp.concatenate(score_wide, axis=0), split_pair(k_ref[here, cols], masks),
            TN, preferred_element_type=jnp.float32,
        ) * inv_root).astype(jnp.bfloat16)
        left_ref[1, here, cols] = (jnp.dot(
            jnp.concatenate(score_wide, axis=1), split_pair(q_ref[here, cols], masks),
            preferred_element_type=jnp.float32,
        ) * inv_root).astype(jnp.bfloat16)
        left_ref[2, here, cols] = jnp.dot(
            jnp.concatenate(prob_wide, axis=1), split_pair(grad_ref[here, cols], masks),
            preferred_element_type=jnp.float32,
        ).astype(jnp.bfloat16)

    fulls, wides = {}, {}
    for index in range(len(places) + 2):
        if index < len(places):
            fulls[index] = grad_probs(*places[index])
        if 0 <= index - 1 < len(places):
            wides[index - 1] = widen(fulls.pop(index - 1), *places[index - 1])
        if 0 <= index - 2:
            contract(wides.pop(index - 2), *places[index - 2])

    total = sum(
        lax.dot_general(weight_ref[...], left_ref[index], NT, preferred_element_type=jnp.float32)
        for index, weight_ref in enumerate((wq_ref, wk_ref, wv_ref))
    ).astype(jnp.bfloat16)
    for col in range(0, channels, BLOCK):
        cols = slice(col, col + BLOCK)
        source = lax.dot_general(
            order_ref[1], total[cols], NT, preferred_element_type=jnp.float32
        )
        result_ref[:, cols] = (
            taps_ref[0:1, cols] * pltpu.roll(source, rows - toks, 0)
            + (1.0 + taps_ref[1:2, cols]) * source
            + taps_ref[2:3, cols] * pltpu.roll(source, toks, 0)
        ).astype(jnp.bfloat16)
    for mask in range(peers):
        start = pl.multiple_of((me ^ mask) * part, part)
        outs[mask][...] = result_ref[pl.ds(start, part), :]


def swap(value, axis, mask):
    return lax.ppermute(value, axis, [(i, i ^ mask) for i in range(lax.axis_size(axis))])


def grant(mebibytes):
    return pltpu.CompilerParams(vmem_limit_bytes=mebibytes << 20)


def on_chip(value):
    return pltpu.with_memory_space_constraint(value, pltpu.VMEM)


def off_chip(value):
    return pltpu.with_memory_space_constraint(value, pltpu.HBM)


def far_first(peers):
    masks = sorted(range(2, peers), key=lambda mask: (-bin(mask >> 1).count("1"), mask & 1, -mask))
    return masks + [1]


def gather_tokens(sent):
    peers = lax.axis_size("orbit")
    _, frame_rows, toks, channels = sent[0].shape
    parts = [sent[0]] + [None] * (peers // 2 - 1)
    for mask in far_first(peers):
        if mask % 2 == 0:
            parts[mask // 2] = swap(sent[mask // 2], "orbit", mask)
    parts = [part.reshape(2, frame_rows * toks, channels) for part in parts]
    own = swap(parts[0][1], "orbit", 1)
    others = pl.pallas_call(
        join_kernel,
        in_specs=[pl.BlockSpec(memory_space=pltpu.VMEM)] * (peers // 2 - 1),
        out_specs=pl.BlockSpec(memory_space=pltpu.VMEM),
        out_shape=pltpu.VMEM((peers // 2 - 1, frame_rows * toks, channels), jnp.bfloat16),
        compiler_params=grant(4),
        name="join",
    )(*map(on_chip, parts[1:]))
    return parts + [own, swap(others, "orbit", 1)]


def spread_frames(blocks):
    peers = len(blocks)
    received = [blocks[0]] + [None] * (peers - 1)
    for mask in far_first(peers):
        received[mask] = swap(blocks[mask], "orbit", mask)
    return received


def tile_terms(value):
    terms = [value]
    for stage in range(lax.axis_size("tile").bit_length() - 1):
        value = sum(terms[1:], terms[0])
        terms = [value, swap(value, "tile", 1 << stage)]
    return terms


def body(tokens, cotangent, w_query, w_key, w_value, conv_taps, conv_bias):
    frame_rows, tile_rows, channels = tokens.shape
    peers = lax.axis_size("orbit")
    me = lax.axis_index("orbit")
    frames = frame_rows * peers
    toks = tile_rows // peers
    rows = frames * toks
    part = frame_rows * toks
    spatial_all = tile_rows * lax.axis_size("tile")
    heads = channels // HEAD_DIM
    me_arg = me.astype(jnp.int32).reshape(1)
    smem = pl.BlockSpec(memory_space=pltpu.SMEM)
    vmem = pl.BlockSpec(memory_space=pltpu.VMEM)
    hbm = pl.BlockSpec(memory_space=pltpu.HBM)
    low = functools.partial(pltpu.VMEM, dtype=jnp.bfloat16)
    sent_shape = low((2, frame_rows, toks, channels))
    split = (frame_rows, peers, toks, channels)

    *sent_tokens, energy, held = pl.pallas_call(
        functools.partial(pack_kernel, peers=peers),
        in_specs=[smem, hbm, hbm],
        out_specs=[vmem] * (peers // 2 + 2),
        out_shape=[sent_shape] * (peers // 2)
        + [pltpu.VMEM((frame_rows, LANES), jnp.float32), low(split)],
        scratch_shapes=[pltpu.SemaphoreType.DMA((peers + frame_rows,))],
        compiler_params=grant(8),
        name="pack",
    )(me_arg, off_chip(tokens.reshape(split)), off_chip(cotangent.reshape(split)))
    token_blocks = gather_tokens(sent_tokens)
    terms = tile_terms(energy)
    sent_grads = pl.pallas_call(
        functools.partial(scale_kernel, peers=peers, count=spatial_all * channels),
        in_specs=[smem] + [vmem] * (1 + len(terms)),
        out_specs=[vmem] * (peers // 2),
        out_shape=[sent_shape] * (peers // 2),
        compiler_params=grant(8),
        cost_estimate=pl.CostEstimate(flops=1 << 34, bytes_accessed=1 << 25, transcendentals=0),
        name="scale",
    )(me_arg, on_chip(held), *map(on_chip, terms))
    grad_blocks = gather_tokens(sent_grads)

    weights = (w_query, w_key, w_value)
    sizes = dict(frames=frames, toks=toks, peers=peers)
    order = on_chip(pl.pallas_call(
        functools.partial(order_kernel, frames=frames, toks=toks),
        out_specs=vmem,
        out_shape=low((2, rows, rows)),
        compiler_params=grant(4),
        name="order",
    )())
    query, key, prob, hidden = pl.pallas_call(
        functools.partial(forward_kernel, **sizes),
        in_specs=[smem] + [vmem] * (7 + peers // 2),
        out_specs=[vmem] * 4,
        out_shape=[low((rows, channels))] * 2
        + [pltpu.VMEM((heads, frames, rows), jnp.float32), low((rows, channels))],
        scratch_shapes=[pltpu.VMEM((rows, channels), jnp.float32)],
        compiler_params=grant(20),
        name="forward",
    )(me_arg, order, conv_taps, conv_bias, *weights[:2], *map(on_chip, token_blocks))
    value = pl.pallas_call(
        value_kernel,
        in_specs=[vmem] * 2,
        out_specs=vmem,
        out_shape=low((rows, channels)),
        compiler_params=grant(8),
        name="value",
    )(on_chip(hidden), weights[2])
    results = pl.pallas_call(
        functools.partial(backward_kernel, **sizes),
        in_specs=[smem] + [vmem] * (11 + peers // 2),
        out_specs=[vmem] * peers,
        out_shape=[low((part, channels))] * peers,
        scratch_shapes=[
            pltpu.VMEM((rows, channels), jnp.bfloat16),
            pltpu.VMEM((3, rows, channels), jnp.bfloat16),
            pltpu.VMEM((rows, channels), jnp.bfloat16),
        ],
        compiler_params=grant(20),
        name="backward",
    )(me_arg, order, conv_taps, *weights, *map(on_chip, (query, key, value, prob)), *map(on_chip, grad_blocks))
    received = [block.reshape(frame_rows, toks, channels) for block in spread_frames(results)]
    early = [mask for mask in range(peers) if bin(mask >> 1).count("1") != 1]
    late = [mask for mask in range(peers) if mask not in early]
    output = None
    for masks in (early, late):
        blocks = [on_chip(received[mask]) for mask in masks]
        output = pl.pallas_call(
            functools.partial(place_kernel, masks=masks),
            in_specs=[smem] + [vmem] * len(masks) + [hbm] * (output is not None),
            out_specs=hbm,
            out_shape=jax.ShapeDtypeStruct(split, jnp.bfloat16),
            scratch_shapes=[pltpu.SemaphoreType.DMA((len(masks),))],
            input_output_aliases={} if output is None else {len(masks) + 1: 0},
            compiler_params=grant(4),
            name="place",
        )(me_arg, *blocks, *([] if output is None else [output]))
    return output.reshape(frame_rows, tile_rows, channels)


def solution(mesh):
    in_specs = (P("orbit", "tile", None), P("orbit", "tile", None), P(), P(), P(), P(), P())
    out_specs = P("orbit", "tile", None)
    return jax.shard_map(body, mesh=mesh, in_specs=in_specs, out_specs=out_specs, check_vma=False)
```

```python
import functools
import math

import jax
import jax.numpy as jnp
from jax import lax
from jax.experimental import pallas as pl
from jax.experimental.pallas import tpu as pltpu
from jax.sharding import PartitionSpec as P


HEAD_DIM = 64
LANES = 128
BLOCK = 256
NT = (((1,), (1,)), ((), ()))
TN = (((0,), (0,)), ((), ()))


def iota(shape, dim):
    return lax.broadcasted_iota(jnp.int32, shape, dim)


def reorder_matrix(frames, toks, to_token_major):
    rows = frames * toks
    out_row = iota((rows, rows), 0)
    in_row = iota((rows, rows), 1)
    if to_token_major:
        source = (out_row % frames) * toks + out_row // frames
    else:
        source = (out_row % toks) * frames + out_row // toks
    return (in_row == source).astype(jnp.float32).astype(jnp.bfloat16)


def half_masks(rows):
    low = (iota((rows, LANES), 1) < HEAD_DIM).astype(jnp.float32)
    return low.astype(jnp.bfloat16), (1.0 - low).astype(jnp.bfloat16)


def split_pair(block, masks):
    return jnp.concatenate([block * masks[0], block * masks[1]], axis=0)


def compact(full, frames):
    token_of = iota((frames, LANES), 1) // frames
    kept = full[:frames]
    for tok in range(1, LANES // frames):
        kept = jnp.where(token_of == tok, full[tok * frames:(tok + 1) * frames], kept)
    return kept


def expand(kept, token_masks):
    return jnp.concatenate([kept * mask for mask in token_masks], axis=0)


def pieces(tokens_ref, outs, me, masks, sems):
    return [
        pltpu.make_async_copy(
            tokens_ref.at[:, me ^ mask], outs[index // 2].at[mask % 2], sems.at[index]
        )
        for index, mask in enumerate(masks)
    ]


def pack_kernel(me_ref, tokens_ref, cotangent_ref, *refs, peers):
    outs = refs[:peers // 2 - 1]
    energy_ref, held_ref, sems = refs[peers // 2 - 1:]
    frame_rows = held_ref.shape[0]
    held = [
        pltpu.make_async_copy(cotangent_ref.at[frame], held_ref.at[frame], sems.at[peers + frame])
        for frame in range(frame_rows)
    ]
    copies = pieces(tokens_ref, outs, me_ref[0], range(2, peers), sems)
    for copy in held + copies:
        copy.start()
    for frame in range(frame_rows):
        held[frame].wait()
        total = jnp.zeros(held_ref.shape[2:], jnp.float32)
        for group in range(peers):
            grad = held_ref[frame, group].astype(jnp.float32)
            total += grad * grad
        energy_ref[frame:frame + 1, :] = jnp.broadcast_to(
            jnp.sum(total, keepdims=True), (1, LANES)
        )
    for copy in copies:
        copy.wait()


def prepare_kernel(me_ref, tokens_ref, sent_ref, order_ref, sems, *, frames, toks):
    copies = pieces(tokens_ref, [sent_ref], me_ref[0], range(2), sems)
    for copy in copies:
        copy.start()
    order_ref[0] = reorder_matrix(frames, toks, True)
    order_ref[1] = reorder_matrix(frames, toks, False)
    for copy in copies:
        copy.wait()


def scale_kernel(me_ref, held_ref, *refs, peers, count):
    energies, outs = refs[:-(peers // 2)], refs[-(peers // 2):]
    me = me_ref[0]
    factor = lax.rsqrt(sum(energy[...] for energy in energies) / count + 1e-06)
    frame_rows = held_ref.shape[0]
    for mask in range(peers):
        for frame in range(frame_rows):
            grad = held_ref[frame, me ^ mask].astype(jnp.float32)
            outs[mask // 2][mask % 2, frame] = (
                grad * factor[frame:frame + 1, :1]
            ).astype(jnp.bfloat16)


def place_kernel(me_ref, *refs, masks):
    out_ref, sems = refs[-2:]
    me = me_ref[0]
    copies = [
        pltpu.make_async_copy(refs[index], out_ref.at[:, me ^ mask], sems.at[index])
        for index, mask in enumerate(masks)
    ]
    for copy in copies:
        copy.start()
    for copy in copies:
        copy.wait()


def join_kernel(*refs):
    for index, pair_ref in enumerate(refs[:-1]):
        refs[-1][index] = pair_ref[1]


def block_of(blocks, mask):
    chip = mask // 2
    if mask % 2 == 0:
        return blocks[chip][0]
    return blocks[-1][chip - 1] if chip else blocks[-2][...]


def forward_kernel(me_ref, order_ref, taps_ref, bias_ref, wq_ref, wk_ref, *refs,
                   frames, toks, peers):
    blocks = refs[:peers // 2 + 2]
    q_ref, k_ref, prob_ref, hidden_ref, source_ref = refs[peers // 2 + 2:]
    rows, channels = hidden_ref.shape
    part = rows // peers
    me = me_ref[0]
    for mask in range(peers):
        start = pl.multiple_of((me ^ mask) * part, part)
        source_ref[pl.ds(start, part), :] = block_of(blocks, mask).astype(jnp.float32)
    for col in range(0, channels, BLOCK):
        cols = slice(col, col + BLOCK)
        source = source_ref[:, cols]
        hidden = (
            taps_ref[0:1, cols] * pltpu.roll(source, toks, 0)
            + (1.0 + taps_ref[1:2, cols]) * source
            + taps_ref[2:3, cols] * pltpu.roll(source, rows - toks, 0)
            + bias_ref[cols].reshape(1, BLOCK)
        ).astype(jnp.bfloat16)
        hidden_ref[:, cols] = jnp.dot(
            order_ref[0], hidden, preferred_element_type=jnp.float32
        ).astype(jnp.bfloat16)

    masks = half_masks(LANES)
    inv_root = 1.0 / math.sqrt(HEAD_DIM)
    for col in range(0, channels, BLOCK):
        block = slice(col, col + BLOCK)
        for weight_ref, out_ref in ((wq_ref, q_ref), (wk_ref, k_ref)):
            out_ref[:, block] = jnp.dot(
                hidden_ref[...], weight_ref[:, block], preferred_element_type=jnp.float32
            ).astype(jnp.bfloat16)
        for start in range(col, col + BLOCK, LANES):
            cols = slice(start, start + LANES)
            for row in range(0, rows, LANES):
                here = slice(row, row + LANES)
                full = lax.dot_general(
                    split_pair(k_ref[here, cols], masks), q_ref[here, cols],
                    NT, preferred_element_type=jnp.float32,
                )
                for head in range(2):
                    scores = compact(full[head * LANES:(head + 1) * LANES], frames) * inv_root
                    expo = jnp.exp(scores - jnp.max(scores, axis=0, keepdims=True))
                    inverse = 1.0 / jnp.sum(expo, axis=0, keepdims=True)
                    prob_ref[start // HEAD_DIM + head, :, here] = expo * inverse


def value_kernel(hidden_ref, wv_ref, v_ref):
    v_ref[...] = jnp.dot(
        hidden_ref[...], wv_ref[...], preferred_element_type=jnp.float32
    ).astype(jnp.bfloat16)


def backward_kernel(me_ref, order_ref, taps_ref, wq_ref, wk_ref, wv_ref, q_ref, k_ref, v_ref,
                    prob_ref, *refs, frames, toks, peers):
    blocks = refs[:peers // 2 + 2]
    outs = refs[peers // 2 + 2:-3]
    grad_ref, left_ref, result_ref = refs[-3:]
    rows, channels = grad_ref.shape
    part = rows // peers
    me = me_ref[0]
    for mask in range(peers):
        start = pl.multiple_of((me ^ mask) * part, part)
        result_ref[pl.ds(start, part), :] = block_of(blocks, mask)
    for col in range(0, channels, BLOCK):
        cols = slice(col, col + BLOCK)
        grad_ref[:, cols] = jnp.dot(
            order_ref[0], result_ref[:, cols], preferred_element_type=jnp.float32
        ).astype(jnp.bfloat16)

    masks = half_masks(LANES)
    token_of = iota((frames, LANES), 1) // frames
    token_masks = [
        (token_of == tok).astype(jnp.float32).astype(jnp.bfloat16) for tok in range(LANES // frames)
    ]
    inv_root = 1.0 / math.sqrt(HEAD_DIM)
    places = [
        (slice(row, row + LANES), slice(col, col + LANES), col // HEAD_DIM)
        for col in range(0, channels, LANES) for row in range(0, rows, LANES)
    ]

    def grad_probs(here, cols, head):
        return lax.dot_general(
            split_pair(v_ref[here, cols], masks), grad_ref[here, cols],
            NT, preferred_element_type=jnp.float32,
        )

    def widen(full, here, cols, head):
        prob_wide, score_wide = [], []
        for half in range(2):
            prob = prob_ref[head + half, :, here]
            prob_low = prob.astype(jnp.bfloat16)
            grad_prob = compact(full[half * LANES:(half + 1) * LANES], frames)
            delta = jnp.sum(prob_low.astype(jnp.float32) * grad_prob, axis=0, keepdims=True)
            d_scores = (prob * (grad_prob - delta)).astype(jnp.bfloat16)
            prob_wide.append(expand(prob_low, token_masks))
            score_wide.append(expand(d_scores, token_masks))
        return prob_wide, score_wide

    def contract(wide, here, cols, head):
        prob_wide, score_wide = wide
        left_ref[0, here, cols] = (lax.dot_general(
            jnp.concatenate(score_wide, axis=0), split_pair(k_ref[here, cols], masks),
            TN, preferred_element_type=jnp.float32,
        ) * inv_root).astype(jnp.bfloat16)
        left_ref[1, here, cols] = (jnp.dot(
            jnp.concatenate(score_wide, axis=1), split_pair(q_ref[here, cols], masks),
            preferred_element_type=jnp.float32,
        ) * inv_root).astype(jnp.bfloat16)
        left_ref[2, here, cols] = jnp.dot(
            jnp.concatenate(prob_wide, axis=1), split_pair(grad_ref[here, cols], masks),
            preferred_element_type=jnp.float32,
        ).astype(jnp.bfloat16)

    fulls, wides = {}, {}
    for index in range(len(places) + 2):
        if index < len(places):
            fulls[index] = grad_probs(*places[index])
        if 0 <= index - 1 < len(places):
            wides[index - 1] = widen(fulls.pop(index - 1), *places[index - 1])
        if 0 <= index - 2:
            contract(wides.pop(index - 2), *places[index - 2])

    total = lax.dot_general(
        jnp.concatenate([wq_ref[...], wk_ref[...], wv_ref[...]], axis=1),
        jnp.concatenate([left_ref[0], left_ref[1], left_ref[2]], axis=1),
        NT, preferred_element_type=jnp.float32,
    ).astype(jnp.bfloat16)
    for col in range(0, channels, BLOCK):
        cols = slice(col, col + BLOCK)
        source = lax.dot_general(
            order_ref[1], total[cols], NT, preferred_element_type=jnp.float32
        )
        result_ref[:, cols] = (
            taps_ref[0:1, cols] * pltpu.roll(source, rows - toks, 0)
            + (1.0 + taps_ref[1:2, cols]) * source
            + taps_ref[2:3, cols] * pltpu.roll(source, toks, 0)
        ).astype(jnp.bfloat16)
    for mask in range(peers):
        start = pl.multiple_of((me ^ mask) * part, part)
        outs[mask][...] = result_ref[pl.ds(start, part), :]


def swap(value, axis, mask):
    return lax.ppermute(value, axis, [(i, i ^ mask) for i in range(lax.axis_size(axis))])


def grant(mebibytes):
    return pltpu.CompilerParams(vmem_limit_bytes=mebibytes << 20)


def on_chip(value):
    return pltpu.with_memory_space_constraint(value, pltpu.VMEM)


def off_chip(value):
    return pltpu.with_memory_space_constraint(value, pltpu.HBM)


def far_first(peers):
    masks = sorted(range(2, peers), key=lambda mask: (-bin(mask >> 1).count("1"), mask & 1, -mask))
    return masks + [1]


def gather_tokens(sent):
    peers = lax.axis_size("orbit")
    _, frame_rows, toks, channels = sent[0].shape
    parts = [sent[0]] + [None] * (peers // 2 - 1)
    for mask in far_first(peers):
        if mask % 2 == 0:
            parts[mask // 2] = swap(sent[mask // 2], "orbit", mask)
    parts = [part.reshape(2, frame_rows * toks, channels) for part in parts]
    own = swap(parts[0][1], "orbit", 1)
    others = pl.pallas_call(
        join_kernel,
        in_specs=[pl.BlockSpec(memory_space=pltpu.VMEM)] * (peers // 2 - 1),
        out_specs=pl.BlockSpec(memory_space=pltpu.VMEM),
        out_shape=pltpu.VMEM((peers // 2 - 1, frame_rows * toks, channels), jnp.bfloat16),
        compiler_params=grant(4),
        name="join",
    )(*map(on_chip, parts[1:]))
    return parts + [own, swap(others, "orbit", 1)]


def spread_frames(blocks):
    peers = len(blocks)
    received = [blocks[0]] + [None] * (peers - 1)
    for mask in far_first(peers):
        received[mask] = swap(blocks[mask], "orbit", mask)
    return received


def tile_terms(value):
    terms = [value]
    for stage in range(lax.axis_size("tile").bit_length() - 1):
        value = sum(terms[1:], terms[0])
        terms = [value, swap(value, "tile", 1 << stage)]
    return terms


def body(tokens, cotangent, w_query, w_key, w_value, conv_taps, conv_bias):
    frame_rows, tile_rows, channels = tokens.shape
    peers = lax.axis_size("orbit")
    me = lax.axis_index("orbit")
    frames = frame_rows * peers
    toks = tile_rows // peers
    rows = frames * toks
    part = frame_rows * toks
    spatial_all = tile_rows * lax.axis_size("tile")
    heads = channels // HEAD_DIM
    me_arg = me.astype(jnp.int32).reshape(1)
    smem = pl.BlockSpec(memory_space=pltpu.SMEM)
    vmem = pl.BlockSpec(memory_space=pltpu.VMEM)
    hbm = pl.BlockSpec(memory_space=pltpu.HBM)
    low = functools.partial(pltpu.VMEM, dtype=jnp.bfloat16)
    sent_shape = low((2, frame_rows, toks, channels))
    split = (frame_rows, peers, toks, channels)

    tokens, cotangent = (off_chip(array.reshape(split)) for array in (tokens, cotangent))
    *sent_tokens, energy, held = pl.pallas_call(
        functools.partial(pack_kernel, peers=peers),
        in_specs=[smem, hbm, hbm],
        out_specs=[vmem] * (peers // 2 + 1),
        out_shape=[sent_shape] * (peers // 2 - 1)
        + [pltpu.VMEM((frame_rows, LANES), jnp.float32), low(split)],
        scratch_shapes=[pltpu.SemaphoreType.DMA((peers + frame_rows,))],
        compiler_params=grant(8),
        name="pack",
    )(me_arg, tokens, cotangent)
    sent_here, order = pl.pallas_call(
        functools.partial(prepare_kernel, frames=frames, toks=toks),
        in_specs=[smem, hbm],
        out_specs=[vmem] * 2,
        out_shape=[sent_shape, low((2, rows, rows))],
        scratch_shapes=[pltpu.SemaphoreType.DMA((2,))],
        compiler_params=grant(4),
        name="prepare",
    )(me_arg, tokens)
    order = on_chip(order)
    sent_tokens = [sent_here, *sent_tokens]
    terms = tile_terms(energy)
    token_blocks = gather_tokens(sent_tokens)
    sent_grads = pl.pallas_call(
        functools.partial(scale_kernel, peers=peers, count=spatial_all * channels),
        in_specs=[smem] + [vmem] * (1 + len(terms)),
        out_specs=[vmem] * (peers // 2),
        out_shape=[sent_shape] * (peers // 2),
        compiler_params=grant(8),
        cost_estimate=pl.CostEstimate(flops=1 << 34, bytes_accessed=1 << 25, transcendentals=0),
        name="scale",
    )(me_arg, on_chip(held), *map(on_chip, terms))
    grad_blocks = gather_tokens(sent_grads)

    weights = (w_query, w_key, w_value)
    sizes = dict(frames=frames, toks=toks, peers=peers)
    query, key, prob, hidden = pl.pallas_call(
        functools.partial(forward_kernel, **sizes),
        in_specs=[smem] + [vmem] * (7 + peers // 2),
        out_specs=[vmem] * 4,
        out_shape=[low((rows, channels))] * 2
        + [pltpu.VMEM((heads, frames, rows), jnp.float32), low((rows, channels))],
        scratch_shapes=[pltpu.VMEM((rows, channels), jnp.float32)],
        compiler_params=grant(20),
        name="forward",
    )(me_arg, order, conv_taps, conv_bias, *weights[:2], *map(on_chip, token_blocks))
    value = pl.pallas_call(
        value_kernel,
        in_specs=[vmem] * 2,
        out_specs=vmem,
        out_shape=low((rows, channels)),
        compiler_params=grant(8),
        name="value",
    )(on_chip(hidden), weights[2])
    results = pl.pallas_call(
        functools.partial(backward_kernel, **sizes),
        in_specs=[smem] + [vmem] * (11 + peers // 2),
        out_specs=[vmem] * peers,
        out_shape=[low((part, channels))] * peers,
        scratch_shapes=[
            pltpu.VMEM((rows, channels), jnp.bfloat16),
            pltpu.VMEM((3, rows, channels), jnp.bfloat16),
            pltpu.VMEM((rows, channels), jnp.bfloat16),
        ],
        compiler_params=grant(20),
        name="backward",
    )(me_arg, order, conv_taps, *weights, *map(on_chip, (query, key, value, prob)), *map(on_chip, grad_blocks))
    received = [block.reshape(frame_rows, toks, channels) for block in spread_frames(results)]
    early = [mask for mask in range(peers) if bin(mask >> 1).count("1") != 1]
    late = [mask for mask in range(peers) if mask not in early]
    output = None
    for masks in (early, late):
        blocks = [on_chip(received[mask]) for mask in masks]
        output = pl.pallas_call(
            functools.partial(place_kernel, masks=masks),
            in_specs=[smem] + [vmem] * len(masks) + [hbm] * (output is not None),
            out_specs=hbm,
            out_shape=jax.ShapeDtypeStruct(split, jnp.bfloat16),
            scratch_shapes=[pltpu.SemaphoreType.DMA((len(masks),))],
            input_output_aliases={} if output is None else {len(masks) + 1: 0},
            compiler_params=grant(4),
            name="place",
        )(me_arg, *blocks, *([] if output is None else [output]))
    return output.reshape(frame_rows, tile_rows, channels)


def solution(mesh):
    in_specs = (P("orbit", "tile", None), P("orbit", "tile", None), P(), P(), P(), P(), P())
    out_specs = P("orbit", "tile", None)
    return jax.shard_map(body, mesh=mesh, in_specs=in_specs, out_specs=out_specs, check_vma=False)
```

```python
import functools
import math

import jax
import jax.numpy as jnp
from jax import lax
from jax.experimental import pallas as pl
from jax.experimental.pallas import tpu as pltpu
from jax.sharding import PartitionSpec as P


HEAD_DIM = 64
LANES = 128
BLOCK = 256
NT = (((1,), (1,)), ((), ()))
TN = (((0,), (0,)), ((), ()))


def iota(shape, dim):
    return lax.broadcasted_iota(jnp.int32, shape, dim)


def reorder_matrix(frames, toks, to_token_major):
    rows = frames * toks
    out_row = iota((rows, rows), 0)
    in_row = iota((rows, rows), 1)
    if to_token_major:
        source = (out_row % frames) * toks + out_row // frames
    else:
        source = (out_row % toks) * frames + out_row // toks
    return (in_row == source).astype(jnp.float32).astype(jnp.bfloat16)


def half_masks(rows):
    low = (iota((rows, LANES), 1) < HEAD_DIM).astype(jnp.float32)
    return low.astype(jnp.bfloat16), (1.0 - low).astype(jnp.bfloat16)


def split_pair(block, masks):
    return jnp.concatenate([block * masks[0], block * masks[1]], axis=0)


def compact(full, frames):
    token_of = iota((frames, LANES), 1) // frames
    kept = full[:frames]
    for tok in range(1, LANES // frames):
        kept = jnp.where(token_of == tok, full[tok * frames:(tok + 1) * frames], kept)
    return kept


def expand(kept, token_masks):
    return jnp.concatenate([kept * mask for mask in token_masks], axis=0)


def pieces(tokens_ref, outs, me, masks, sems):
    return [
        pltpu.make_async_copy(
            tokens_ref.at[:, me ^ mask], outs[index // 2].at[mask % 2], sems.at[index]
        )
        for index, mask in enumerate(masks)
    ]


def pack_kernel(me_ref, tokens_ref, cotangent_ref, *refs, peers):
    outs = refs[:peers // 2 - 1]
    energy_ref, held_ref, sems = refs[peers // 2 - 1:]
    frame_rows = held_ref.shape[0]
    held = pltpu.make_async_copy(cotangent_ref, held_ref, sems.at[peers])
    copies = pieces(tokens_ref, outs, me_ref[0], range(2, peers), sems)
    for copy in [held] + copies:
        copy.start()
    held.wait()
    partial = []
    for frame in range(frame_rows):
        total = jnp.zeros(held_ref.shape[2:], jnp.float32)
        for group in range(peers):
            grad = held_ref[frame, group].astype(jnp.float32)
            total += grad * grad
        lanes = sum(total[:, col:col + LANES] for col in range(0, total.shape[1], LANES))
        partial.append(jnp.sum(lanes, axis=0, keepdims=True))
    energy_ref[...] = jnp.broadcast_to(
        jnp.sum(jnp.concatenate(partial, axis=0), axis=1, keepdims=True), energy_ref.shape
    )
    for copy in copies:
        copy.wait()


def prepare_kernel(me_ref, tokens_ref, sent_ref, order_ref, sems, *, frames, toks):
    copies = pieces(tokens_ref, [sent_ref], me_ref[0], range(2), sems)
    for copy in copies:
        copy.start()
    order_ref[0] = reorder_matrix(frames, toks, True)
    order_ref[1] = reorder_matrix(frames, toks, False)
    for copy in copies:
        copy.wait()


def scale_kernel(me_ref, held_ref, *refs, peers, count):
    energies, outs = refs[:-(peers // 2)], refs[-(peers // 2):]
    me = me_ref[0]
    factor = lax.rsqrt(sum(energy[...] for energy in energies) / count + 1e-06)
    frame_rows = held_ref.shape[0]
    for mask in range(peers):
        for frame in range(frame_rows):
            grad = held_ref[frame, me ^ mask].astype(jnp.float32)
            outs[mask // 2][mask % 2, frame] = (
                grad * factor[frame:frame + 1, :1]
            ).astype(jnp.bfloat16)


def place_kernel(me_ref, *refs, masks):
    out_ref, sems = refs[-2:]
    me = me_ref[0]
    copies = [
        pltpu.make_async_copy(refs[index], out_ref.at[:, me ^ mask], sems.at[index])
        for index, mask in enumerate(masks)
    ]
    for copy in copies:
        copy.start()
    for copy in copies:
        copy.wait()


def join_kernel(*refs):
    for index, pair_ref in enumerate(refs[:-1]):
        refs[-1][index] = pair_ref[1]


def block_of(blocks, mask):
    chip = mask // 2
    if mask % 2 == 0:
        return blocks[chip][0]
    return blocks[-1][chip - 1] if chip else blocks[-2][...]


def forward_kernel(me_ref, order_ref, taps_ref, bias_ref, wq_ref, wk_ref, *refs,
                   frames, toks, peers):
    blocks = refs[:peers // 2 + 2]
    q_ref, k_ref, prob_ref, hidden_ref, source_ref = refs[peers // 2 + 2:]
    rows, channels = hidden_ref.shape
    part = rows // peers
    me = me_ref[0]
    for mask in range(peers):
        start = pl.multiple_of((me ^ mask) * part, part)
        source_ref[pl.ds(start, part), :] = block_of(blocks, mask).astype(jnp.float32)
    for col in range(0, channels, BLOCK):
        cols = slice(col, col + BLOCK)
        source = source_ref[:, cols]
        hidden = (
            taps_ref[0:1, cols] * pltpu.roll(source, toks, 0)
            + (1.0 + taps_ref[1:2, cols]) * source
            + taps_ref[2:3, cols] * pltpu.roll(source, rows - toks, 0)
            + bias_ref[cols].reshape(1, BLOCK)
        ).astype(jnp.bfloat16)
        hidden_ref[:, cols] = jnp.dot(
            order_ref[0], hidden, preferred_element_type=jnp.float32
        ).astype(jnp.bfloat16)

    masks = half_masks(LANES)
    inv_root = 1.0 / math.sqrt(HEAD_DIM)
    for col in range(0, channels, BLOCK):
        block = slice(col, col + BLOCK)
        for weight_ref, out_ref in ((wq_ref, q_ref), (wk_ref, k_ref)):
            out_ref[:, block] = jnp.dot(
                hidden_ref[...], weight_ref[:, block], preferred_element_type=jnp.float32
            ).astype(jnp.bfloat16)
        for start in range(col, col + BLOCK, LANES):
            cols = slice(start, start + LANES)
            for row in range(0, rows, LANES):
                here = slice(row, row + LANES)
                full = lax.dot_general(
                    split_pair(k_ref[here, cols], masks), q_ref[here, cols],
                    NT, preferred_element_type=jnp.float32,
                )
                for head in range(2):
                    scores = compact(full[head * LANES:(head + 1) * LANES], frames) * inv_root
                    expo = jnp.exp(scores - jnp.max(scores, axis=0, keepdims=True))
                    inverse = 1.0 / jnp.sum(expo, axis=0, keepdims=True)
                    prob_ref[start // HEAD_DIM + head, :, here] = expo * inverse


def value_kernel(hidden_ref, wv_ref, v_ref):
    v_ref[...] = jnp.dot(
        hidden_ref[...], wv_ref[...], preferred_element_type=jnp.float32
    ).astype(jnp.bfloat16)


def backward_kernel(me_ref, order_ref, taps_ref, wq_ref, wk_ref, wv_ref, q_ref, k_ref, v_ref,
                    prob_ref, *refs, frames, toks, peers):
    blocks = refs[:peers // 2 + 2]
    outs = refs[peers // 2 + 2:-3]
    grad_ref, left_ref, result_ref = refs[-3:]
    rows, channels = grad_ref.shape
    part = rows // peers
    me = me_ref[0]
    for mask in range(peers):
        start = pl.multiple_of((me ^ mask) * part, part)
        result_ref[pl.ds(start, part), :] = block_of(blocks, mask)
    for col in range(0, channels, BLOCK):
        cols = slice(col, col + BLOCK)
        grad_ref[:, cols] = jnp.dot(
            order_ref[0], result_ref[:, cols], preferred_element_type=jnp.float32
        ).astype(jnp.bfloat16)

    masks = half_masks(LANES)
    token_of = iota((frames, LANES), 1) // frames
    token_masks = [
        (token_of == tok).astype(jnp.float32).astype(jnp.bfloat16) for tok in range(LANES // frames)
    ]
    inv_root = 1.0 / math.sqrt(HEAD_DIM)
    places = [
        (slice(row, row + LANES), slice(col, col + LANES), col // HEAD_DIM)
        for col in range(0, channels, LANES) for row in range(0, rows, LANES)
    ]

    def grad_probs(here, cols, head):
        return lax.dot_general(
            split_pair(v_ref[here, cols], masks), grad_ref[here, cols],
            NT, preferred_element_type=jnp.float32,
        )

    def widen(full, here, cols, head):
        prob_wide, score_wide = [], []
        for half in range(2):
            prob = prob_ref[head + half, :, here]
            prob_low = prob.astype(jnp.bfloat16)
            grad_prob = compact(full[half * LANES:(half + 1) * LANES], frames)
            delta = jnp.sum(prob_low.astype(jnp.float32) * grad_prob, axis=0, keepdims=True)
            d_scores = (prob * (grad_prob - delta)).astype(jnp.bfloat16)
            prob_wide.append(expand(prob_low, token_masks))
            score_wide.append(expand(d_scores, token_masks))
        return prob_wide, score_wide

    def contract(wide, here, cols, head):
        prob_wide, score_wide = wide
        left_ref[0, here, cols] = (lax.dot_general(
            jnp.concatenate(score_wide, axis=0), split_pair(k_ref[here, cols], masks),
            TN, preferred_element_type=jnp.float32,
        ) * inv_root).astype(jnp.bfloat16)
        left_ref[1, here, cols] = (jnp.dot(
            jnp.concatenate(score_wide, axis=1), split_pair(q_ref[here, cols], masks),
            preferred_element_type=jnp.float32,
        ) * inv_root).astype(jnp.bfloat16)
        left_ref[2, here, cols] = jnp.dot(
            jnp.concatenate(prob_wide, axis=1), split_pair(grad_ref[here, cols], masks),
            preferred_element_type=jnp.float32,
        ).astype(jnp.bfloat16)

    fulls, wides = {}, {}
    for index in range(len(places) + 2):
        if index < len(places):
            fulls[index] = grad_probs(*places[index])
        if 0 <= index - 1 < len(places):
            wides[index - 1] = widen(fulls.pop(index - 1), *places[index - 1])
        if 0 <= index - 2:
            contract(wides.pop(index - 2), *places[index - 2])

    total = lax.dot_general(
        jnp.concatenate([wq_ref[...], wk_ref[...], wv_ref[...]], axis=1),
        jnp.concatenate([left_ref[0], left_ref[1], left_ref[2]], axis=1),
        NT, preferred_element_type=jnp.float32,
    ).astype(jnp.bfloat16)
    for col in range(0, channels, BLOCK):
        cols = slice(col, col + BLOCK)
        source = lax.dot_general(
            order_ref[1], total[cols], NT, preferred_element_type=jnp.float32
        )
        result_ref[:, cols] = (
            taps_ref[0:1, cols] * pltpu.roll(source, rows - toks, 0)
            + (1.0 + taps_ref[1:2, cols]) * source
            + taps_ref[2:3, cols] * pltpu.roll(source, toks, 0)
        ).astype(jnp.bfloat16)
    for mask in range(peers):
        start = pl.multiple_of((me ^ mask) * part, part)
        outs[mask][...] = result_ref[pl.ds(start, part), :]


def swap(value, axis, mask):
    return lax.ppermute(value, axis, [(i, i ^ mask) for i in range(lax.axis_size(axis))])


def grant(mebibytes):
    return pltpu.CompilerParams(vmem_limit_bytes=mebibytes << 20)


def on_chip(value):
    return pltpu.with_memory_space_constraint(value, pltpu.VMEM)


def off_chip(value):
    return pltpu.with_memory_space_constraint(value, pltpu.HBM)


def far_first(peers):
    masks = sorted(range(2, peers), key=lambda mask: (-bin(mask >> 1).count("1"), mask & 1, -mask))
    return masks + [1]


def gather_tokens(sent):
    peers = lax.axis_size("orbit")
    _, frame_rows, toks, channels = sent[0].shape
    parts = [sent[0]] + [None] * (peers // 2 - 1)
    for mask in far_first(peers):
        if mask % 2 == 0:
            parts[mask // 2] = swap(sent[mask // 2], "orbit", mask)
    parts = [part.reshape(2, frame_rows * toks, channels) for part in parts]
    own = swap(parts[0][1], "orbit", 1)
    others = pl.pallas_call(
        join_kernel,
        in_specs=[pl.BlockSpec(memory_space=pltpu.VMEM)] * (peers // 2 - 1),
        out_specs=pl.BlockSpec(memory_space=pltpu.VMEM),
        out_shape=pltpu.VMEM((peers // 2 - 1, frame_rows * toks, channels), jnp.bfloat16),
        compiler_params=grant(4),
        name="join",
    )(*map(on_chip, parts[1:]))
    return parts + [own, swap(others, "orbit", 1)]


def spread_frames(blocks):
    peers = len(blocks)
    received = [blocks[0]] + [None] * (peers - 1)
    for mask in far_first(peers):
        received[mask] = swap(blocks[mask], "orbit", mask)
    return received


def tile_terms(value):
    terms = [value]
    for stage in range(lax.axis_size("tile").bit_length() - 1):
        value = sum(terms[1:], terms[0])
        terms = [value, swap(value, "tile", 1 << stage)]
    return terms


def body(tokens, cotangent, w_query, w_key, w_value, conv_taps, conv_bias):
    frame_rows, tile_rows, channels = tokens.shape
    peers = lax.axis_size("orbit")
    me = lax.axis_index("orbit")
    frames = frame_rows * peers
    toks = tile_rows // peers
    rows = frames * toks
    part = frame_rows * toks
    spatial_all = tile_rows * lax.axis_size("tile")
    heads = channels // HEAD_DIM
    me_arg = me.astype(jnp.int32).reshape(1)
    smem = pl.BlockSpec(memory_space=pltpu.SMEM)
    vmem = pl.BlockSpec(memory_space=pltpu.VMEM)
    hbm = pl.BlockSpec(memory_space=pltpu.HBM)
    low = functools.partial(pltpu.VMEM, dtype=jnp.bfloat16)
    sent_shape = low((2, frame_rows, toks, channels))
    split = (frame_rows, peers, toks, channels)

    tokens, cotangent = (off_chip(array.reshape(split)) for array in (tokens, cotangent))
    *sent_tokens, energy, held = pl.pallas_call(
        functools.partial(pack_kernel, peers=peers),
        in_specs=[smem, hbm, hbm],
        out_specs=[vmem] * (peers // 2 + 1),
        out_shape=[sent_shape] * (peers // 2 - 1)
        + [pltpu.VMEM((frame_rows, LANES), jnp.float32), low(split)],
        scratch_shapes=[pltpu.SemaphoreType.DMA((peers + 1,))],
        compiler_params=grant(8),
        name="pack",
    )(me_arg, tokens, cotangent)
    sent_here, order = pl.pallas_call(
        functools.partial(prepare_kernel, frames=frames, toks=toks),
        in_specs=[smem, hbm],
        out_specs=[vmem] * 2,
        out_shape=[sent_shape, low((2, rows, rows))],
        scratch_shapes=[pltpu.SemaphoreType.DMA((2,))],
        compiler_params=grant(4),
        name="prepare",
    )(me_arg, tokens)
    order = on_chip(order)
    sent_tokens = [sent_here, *sent_tokens]
    terms = tile_terms(energy)
    token_blocks = gather_tokens(sent_tokens)
    sent_grads = pl.pallas_call(
        functools.partial(scale_kernel, peers=peers, count=spatial_all * channels),
        in_specs=[smem] + [vmem] * (1 + len(terms)),
        out_specs=[vmem] * (peers // 2),
        out_shape=[sent_shape] * (peers // 2),
        compiler_params=grant(8),
        cost_estimate=pl.CostEstimate(flops=1 << 34, bytes_accessed=1 << 25, transcendentals=0),
        name="scale",
    )(me_arg, on_chip(held), *map(on_chip, terms))
    grad_blocks = gather_tokens(sent_grads)

    weights = (w_query, w_key, w_value)
    sizes = dict(frames=frames, toks=toks, peers=peers)
    query, key, prob, hidden = pl.pallas_call(
        functools.partial(forward_kernel, **sizes),
        in_specs=[smem] + [vmem] * (7 + peers // 2),
        out_specs=[vmem] * 4,
        out_shape=[low((rows, channels))] * 2
        + [pltpu.VMEM((heads, frames, rows), jnp.float32), low((rows, channels))],
        scratch_shapes=[pltpu.VMEM((rows, channels), jnp.float32)],
        compiler_params=grant(20),
        name="forward",
    )(me_arg, order, conv_taps, conv_bias, *weights[:2], *map(on_chip, token_blocks))
    value = pl.pallas_call(
        value_kernel,
        in_specs=[vmem] * 2,
        out_specs=vmem,
        out_shape=low((rows, channels)),
        compiler_params=grant(8),
        name="value",
    )(on_chip(hidden), weights[2])
    results = pl.pallas_call(
        functools.partial(backward_kernel, **sizes),
        in_specs=[smem] + [vmem] * (11 + peers // 2),
        out_specs=[vmem] * peers,
        out_shape=[low((part, channels))] * peers,
        scratch_shapes=[
            pltpu.VMEM((rows, channels), jnp.bfloat16),
            pltpu.VMEM((3, rows, channels), jnp.bfloat16),
            pltpu.VMEM((rows, channels), jnp.bfloat16),
        ],
        compiler_params=grant(20),
        name="backward",
    )(me_arg, order, conv_taps, *weights, *map(on_chip, (query, key, value, prob)), *map(on_chip, grad_blocks))
    received = [block.reshape(frame_rows, toks, channels) for block in spread_frames(results)]
    early = [mask for mask in range(peers) if bin(mask >> 1).count("1") != 1]
    late = [mask for mask in range(peers) if mask not in early]
    output = None
    for masks in (early, late):
        blocks = [on_chip(received[mask]) for mask in masks]
        output = pl.pallas_call(
            functools.partial(place_kernel, masks=masks),
            in_specs=[smem] + [vmem] * len(masks) + [hbm] * (output is not None),
            out_specs=hbm,
            out_shape=jax.ShapeDtypeStruct(split, jnp.bfloat16),
            scratch_shapes=[pltpu.SemaphoreType.DMA((len(masks),))],
            input_output_aliases={} if output is None else {len(masks) + 1: 0},
            compiler_params=grant(4),
            name="place",
        )(me_arg, *blocks, *([] if output is None else [output]))
    return output.reshape(frame_rows, tile_rows, channels)


def solution(mesh):
    in_specs = (P("orbit", "tile", None), P("orbit", "tile", None), P(), P(), P(), P(), P())
    out_specs = P("orbit", "tile", None)
    return jax.shard_map(body, mesh=mesh, in_specs=in_specs, out_specs=out_specs, check_vma=False)
```

```python
import functools
import math

import jax
import jax.numpy as jnp
from jax import lax
from jax.experimental import pallas as pl
from jax.experimental.pallas import tpu as pltpu
from jax.sharding import PartitionSpec as P


HEAD_DIM = 64
LANES = 128
BLOCK = 256
NT = (((1,), (1,)), ((), ()))
TN = (((0,), (0,)), ((), ()))


def iota(shape, dim):
    return lax.broadcasted_iota(jnp.int32, shape, dim)


def reorder_matrix(frames, toks, to_token_major):
    rows = frames * toks
    out_row = iota((rows, rows), 0)
    in_row = iota((rows, rows), 1)
    if to_token_major:
        source = (out_row % frames) * toks + out_row // frames
    else:
        source = (out_row % toks) * frames + out_row // toks
    return (in_row == source).astype(jnp.float32).astype(jnp.bfloat16)


def half_masks(rows):
    low = (iota((rows, LANES), 1) < HEAD_DIM).astype(jnp.float32)
    return low.astype(jnp.bfloat16), (1.0 - low).astype(jnp.bfloat16)


def split_pair(block, masks):
    return jnp.concatenate([block * masks[0], block * masks[1]], axis=0)


def compact(full, frames):
    token_of = iota((frames, LANES), 1) // frames
    kept = full[:frames]
    for tok in range(1, LANES // frames):
        kept = jnp.where(token_of == tok, full[tok * frames:(tok + 1) * frames], kept)
    return kept


def expand(kept, token_masks):
    return jnp.concatenate([kept * mask for mask in token_masks], axis=0)


def pieces(tokens_ref, outs, me, masks, sems):
    return [
        pltpu.make_async_copy(
            tokens_ref.at[:, me ^ mask], outs[index // 2].at[mask % 2], sems.at[index]
        )
        for index, mask in enumerate(masks)
    ]


def pack_kernel(me_ref, tokens_ref, cotangent_ref, *refs, peers):
    outs = refs[:peers // 2 - 1]
    energy_ref, held_ref, sems = refs[peers // 2 - 1:]
    frame_rows = held_ref.shape[0]
    held = pltpu.make_async_copy(cotangent_ref, held_ref, sems.at[peers])
    copies = pieces(tokens_ref, outs, me_ref[0], range(2, peers), sems)
    for copy in [held] + copies:
        copy.start()
    held.wait()
    partial = []
    for frame in range(frame_rows):
        total = jnp.zeros(held_ref.shape[2:], jnp.float32)
        for group in range(peers):
            grad = held_ref[frame, group].astype(jnp.float32)
            total += grad * grad
        lanes = sum(total[:, col:col + LANES] for col in range(0, total.shape[1], LANES))
        partial.append(jnp.sum(lanes, axis=0, keepdims=True))
    energy_ref[...] = jnp.broadcast_to(
        jnp.sum(jnp.concatenate(partial, axis=0), axis=1, keepdims=True), energy_ref.shape
    )
    for copy in copies:
        copy.wait()


def prepare_kernel(me_ref, tokens_ref, sent_ref, order_ref, sems, *, frames, toks):
    copies = pieces(tokens_ref, [sent_ref], me_ref[0], range(2), sems)
    for copy in copies:
        copy.start()
    order_ref[0] = reorder_matrix(frames, toks, True)
    order_ref[1] = reorder_matrix(frames, toks, False)
    for copy in copies:
        copy.wait()


def scale_kernel(me_ref, held_ref, *refs, peers, count):
    energies, outs = refs[:-(peers // 2)], refs[-(peers // 2):]
    me = me_ref[0]
    factor = lax.rsqrt(sum(energy[...] for energy in energies) / count + 1e-06)
    frame_rows = held_ref.shape[0]
    for mask in range(peers):
        for frame in range(frame_rows):
            grad = held_ref[frame, me ^ mask].astype(jnp.float32)
            outs[mask // 2][mask % 2, frame] = (
                grad * factor[frame:frame + 1, :1]
            ).astype(jnp.bfloat16)


def place_kernel(me_ref, *refs, masks):
    out_ref, sems = refs[-2:]
    me = me_ref[0]
    copies = [
        pltpu.make_async_copy(refs[index], out_ref.at[:, me ^ mask], sems.at[index])
        for index, mask in enumerate(masks)
    ]
    for copy in copies:
        copy.start()
    for copy in copies:
        copy.wait()


def join_kernel(*refs):
    for index, pair_ref in enumerate(refs[:-1]):
        refs[-1][index] = pair_ref[1]


def block_of(blocks, mask):
    chip = mask // 2
    if mask % 2 == 0:
        return blocks[chip][0]
    return blocks[-1][chip - 1] if chip else blocks[-2][...]


def forward_kernel(me_ref, order_ref, taps_ref, bias_ref, wq_ref, wk_ref, *refs,
                   frames, toks, peers):
    blocks = refs[:peers // 2 + 2]
    q_ref, k_ref, prob_ref, hidden_ref, source_ref = refs[peers // 2 + 2:]
    rows, channels = hidden_ref.shape
    part = rows // peers
    me = me_ref[0]
    for mask in range(peers):
        start = pl.multiple_of((me ^ mask) * part, part)
        source_ref[pl.ds(start, part), :] = block_of(blocks, mask).astype(jnp.float32)
    for col in range(0, channels, BLOCK):
        cols = slice(col, col + BLOCK)
        source = source_ref[:, cols]
        hidden = (
            taps_ref[0:1, cols] * pltpu.roll(source, toks, 0)
            + (1.0 + taps_ref[1:2, cols]) * source
            + taps_ref[2:3, cols] * pltpu.roll(source, rows - toks, 0)
            + bias_ref[cols].reshape(1, BLOCK)
        ).astype(jnp.bfloat16)
        hidden_ref[:, cols] = jnp.dot(
            order_ref[0], hidden, preferred_element_type=jnp.float32
        ).astype(jnp.bfloat16)

    masks = half_masks(LANES)
    inv_root = 1.0 / math.sqrt(HEAD_DIM)
    for col in range(0, channels, BLOCK):
        block = slice(col, col + BLOCK)
        for weight_ref, out_ref in ((wq_ref, q_ref), (wk_ref, k_ref)):
            out_ref[:, block] = jnp.dot(
                hidden_ref[...], weight_ref[:, block], preferred_element_type=jnp.float32
            ).astype(jnp.bfloat16)
        for start in range(col, col + BLOCK, LANES):
            cols = slice(start, start + LANES)
            for row in range(0, rows, LANES):
                here = slice(row, row + LANES)
                full = lax.dot_general(
                    split_pair(k_ref[here, cols], masks), q_ref[here, cols],
                    NT, preferred_element_type=jnp.float32,
                )
                for head in range(2):
                    scores = compact(full[head * LANES:(head + 1) * LANES], frames) * inv_root
                    expo = jnp.exp(scores - jnp.max(scores, axis=0, keepdims=True))
                    inverse = 1.0 / jnp.sum(expo, axis=0, keepdims=True)
                    prob_ref[start // HEAD_DIM + head, :, here] = expo * inverse


def value_kernel(hidden_ref, wv_ref, v_ref):
    v_ref[...] = jnp.dot(
        hidden_ref[...], wv_ref[...], preferred_element_type=jnp.float32
    ).astype(jnp.bfloat16)


def backward_kernel(me_ref, order_ref, taps_ref, wq_ref, wk_ref, wv_ref, q_ref, k_ref, v_ref,
                    prob_ref, *refs, frames, toks, peers):
    blocks = refs[:peers // 2 + 2]
    outs = refs[peers // 2 + 2:-3]
    grad_ref, left_ref, result_ref = refs[-3:]
    rows, channels = grad_ref.shape
    part = rows // peers
    me = me_ref[0]
    for mask in range(peers):
        start = pl.multiple_of((me ^ mask) * part, part)
        result_ref[pl.ds(start, part), :] = block_of(blocks, mask)
    for col in range(0, channels, BLOCK):
        cols = slice(col, col + BLOCK)
        grad_ref[:, cols] = jnp.dot(
            order_ref[0], result_ref[:, cols], preferred_element_type=jnp.float32
        ).astype(jnp.bfloat16)

    masks = half_masks(LANES)
    token_of = iota((frames, LANES), 1) // frames
    token_masks = [
        (token_of == tok).astype(jnp.float32).astype(jnp.bfloat16) for tok in range(LANES // frames)
    ]
    inv_root = 1.0 / math.sqrt(HEAD_DIM)
    places = [
        (slice(row, row + LANES), slice(col, col + LANES), col // HEAD_DIM)
        for col in range(0, channels, LANES) for row in range(0, rows, LANES)
    ]

    def grad_probs(here, cols, head):
        return lax.dot_general(
            split_pair(v_ref[here, cols], masks), grad_ref[here, cols],
            NT, preferred_element_type=jnp.float32,
        )

    def widen(full, here, cols, head):
        prob_wide, score_wide = [], []
        for half in range(2):
            prob = prob_ref[head + half, :, here]
            prob_low = prob.astype(jnp.bfloat16)
            grad_prob = compact(full[half * LANES:(half + 1) * LANES], frames)
            delta = jnp.sum(prob_low.astype(jnp.float32) * grad_prob, axis=0, keepdims=True)
            d_scores = (prob * (grad_prob - delta)).astype(jnp.bfloat16)
            prob_wide.append(expand(prob_low, token_masks))
            score_wide.append(expand(d_scores, token_masks))
        return prob_wide, score_wide

    def contract(wide, here, cols, head):
        prob_wide, score_wide = wide
        left_ref[0, here, cols] = (lax.dot_general(
            jnp.concatenate(score_wide, axis=0), split_pair(k_ref[here, cols], masks),
            TN, preferred_element_type=jnp.float32,
        ) * inv_root).astype(jnp.bfloat16)
        left_ref[1, here, cols] = (jnp.dot(
            jnp.concatenate(score_wide, axis=1), split_pair(q_ref[here, cols], masks),
            preferred_element_type=jnp.float32,
        ) * inv_root).astype(jnp.bfloat16)
        left_ref[2, here, cols] = jnp.dot(
            jnp.concatenate(prob_wide, axis=1), split_pair(grad_ref[here, cols], masks),
            preferred_element_type=jnp.float32,
        ).astype(jnp.bfloat16)

    fulls, wides = {}, {}
    for index in range(len(places) + 2):
        if index < len(places):
            fulls[index] = grad_probs(*places[index])
        if 0 <= index - 1 < len(places):
            wides[index - 1] = widen(fulls.pop(index - 1), *places[index - 1])
        if 0 <= index - 2:
            contract(wides.pop(index - 2), *places[index - 2])

    total = lax.dot_general(
        jnp.concatenate([wq_ref[...], wk_ref[...], wv_ref[...]], axis=1),
        jnp.concatenate([left_ref[0], left_ref[1], left_ref[2]], axis=1),
        NT, preferred_element_type=jnp.float32,
    ).astype(jnp.bfloat16)
    for col in range(0, channels, BLOCK):
        cols = slice(col, col + BLOCK)
        source = lax.dot_general(
            order_ref[1], total[cols], NT, preferred_element_type=jnp.float32
        )
        result_ref[:, cols] = (
            taps_ref[0:1, cols] * pltpu.roll(source, rows - toks, 0)
            + (1.0 + taps_ref[1:2, cols]) * source
            + taps_ref[2:3, cols] * pltpu.roll(source, toks, 0)
        ).astype(jnp.bfloat16)
    for mask in range(peers):
        start = pl.multiple_of((me ^ mask) * part, part)
        outs[mask][...] = result_ref[pl.ds(start, part), :]


def swap(value, axis, mask):
    return lax.ppermute(value, axis, [(i, i ^ mask) for i in range(lax.axis_size(axis))])


def grant(mebibytes):
    return pltpu.CompilerParams(vmem_limit_bytes=mebibytes << 20)


def on_chip(value):
    return pltpu.with_memory_space_constraint(value, pltpu.VMEM)


def off_chip(value):
    return pltpu.with_memory_space_constraint(value, pltpu.HBM)


def far_first(peers):
    masks = sorted(range(2, peers), key=lambda mask: (-bin(mask >> 1).count("1"), mask & 1, -mask))
    return masks + [1]


def gather_tokens(sent):
    peers = lax.axis_size("orbit")
    _, frame_rows, toks, channels = sent[0].shape
    parts = [sent[0]] + [None] * (peers // 2 - 1)
    for mask in far_first(peers):
        if mask % 2 == 0:
            parts[mask // 2] = swap(sent[mask // 2], "orbit", mask)
    parts = [part.reshape(2, frame_rows * toks, channels) for part in parts]
    own = swap(parts[0][1], "orbit", 1)
    others = pl.pallas_call(
        join_kernel,
        in_specs=[pl.BlockSpec(memory_space=pltpu.VMEM)] * (peers // 2 - 1),
        out_specs=pl.BlockSpec(memory_space=pltpu.VMEM),
        out_shape=pltpu.VMEM((peers // 2 - 1, frame_rows * toks, channels), jnp.bfloat16),
        compiler_params=grant(4),
        name="join",
    )(*map(on_chip, parts[1:]))
    return parts + [own, swap(others, "orbit", 1)]


def spread_frames(blocks):
    peers = len(blocks)
    received = [blocks[0]] + [None] * (peers - 1)
    for mask in far_first(peers):
        received[mask] = swap(blocks[mask], "orbit", mask)
    return received


def tile_terms(value):
    terms = [value]
    for stage in range(lax.axis_size("tile").bit_length() - 1):
        value = sum(terms[1:], terms[0])
        terms = [value, swap(value, "tile", 1 << stage)]
    return terms


def body(tokens, cotangent, w_query, w_key, w_value, conv_taps, conv_bias):
    frame_rows, tile_rows, channels = tokens.shape
    peers = lax.axis_size("orbit")
    me = lax.axis_index("orbit")
    frames = frame_rows * peers
    toks = tile_rows // peers
    rows = frames * toks
    part = frame_rows * toks
    spatial_all = tile_rows * lax.axis_size("tile")
    heads = channels // HEAD_DIM
    me_arg = me.astype(jnp.int32).reshape(1)
    smem = pl.BlockSpec(memory_space=pltpu.SMEM)
    vmem = pl.BlockSpec(memory_space=pltpu.VMEM)
    hbm = pl.BlockSpec(memory_space=pltpu.HBM)
    low = functools.partial(pltpu.VMEM, dtype=jnp.bfloat16)
    sent_shape = low((2, frame_rows, toks, channels))
    split = (frame_rows, peers, toks, channels)

    tokens, cotangent = (off_chip(array.reshape(split)) for array in (tokens, cotangent))
    *sent_tokens, energy, held = pl.pallas_call(
        functools.partial(pack_kernel, peers=peers),
        in_specs=[smem, hbm, hbm],
        out_specs=[vmem] * (peers // 2 + 1),
        out_shape=[sent_shape] * (peers // 2 - 1)
        + [pltpu.VMEM((frame_rows, LANES), jnp.float32), low(split)],
        scratch_shapes=[pltpu.SemaphoreType.DMA((peers + 1,))],
        compiler_params=grant(8),
        name="pack",
    )(me_arg, tokens, cotangent)
    sent_here, order = pl.pallas_call(
        functools.partial(prepare_kernel, frames=frames, toks=toks),
        in_specs=[smem, hbm],
        out_specs=[vmem] * 2,
        out_shape=[sent_shape, low((2, rows, rows))],
        scratch_shapes=[pltpu.SemaphoreType.DMA((2,))],
        compiler_params=grant(4),
        name="prepare",
    )(me_arg, tokens)
    order = on_chip(order)
    sent_tokens = [sent_here, *sent_tokens]
    terms = tile_terms(energy)
    token_blocks = gather_tokens(sent_tokens)
    sent_grads = pl.pallas_call(
        functools.partial(scale_kernel, peers=peers, count=spatial_all * channels),
        in_specs=[smem] + [vmem] * (1 + len(terms)),
        out_specs=[vmem] * (peers // 2),
        out_shape=[sent_shape] * (peers // 2),
        compiler_params=grant(8),
        cost_estimate=pl.CostEstimate(flops=1 << 34, bytes_accessed=1 << 25, transcendentals=0),
        name="scale",
    )(me_arg, on_chip(held), *map(on_chip, terms))
    grad_blocks = gather_tokens(sent_grads)

    weights = (w_query, w_key, w_value)
    sizes = dict(frames=frames, toks=toks, peers=peers)
    query, key, prob, hidden = pl.pallas_call(
        functools.partial(forward_kernel, **sizes),
        in_specs=[smem] + [vmem] * (7 + peers // 2),
        out_specs=[vmem] * 4,
        out_shape=[low((rows, channels))] * 2
        + [pltpu.VMEM((heads, frames, rows), jnp.float32), low((rows, channels))],
        scratch_shapes=[pltpu.VMEM((rows, channels), jnp.float32)],
        compiler_params=pltpu.CompilerParams(vmem_limit_bytes=20 << 20),
        name="forward",
    )(me_arg, order, conv_taps, conv_bias, *weights[:2], *map(on_chip, token_blocks))
    value = pl.pallas_call(
        value_kernel,
        in_specs=[vmem] * 2,
        out_specs=vmem,
        out_shape=low((rows, channels)),
        compiler_params=grant(8),
        name="value",
    )(on_chip(hidden), weights[2])
    results = pl.pallas_call(
        functools.partial(backward_kernel, **sizes),
        in_specs=[smem] + [vmem] * (11 + peers // 2),
        out_specs=[vmem] * peers,
        out_shape=[low((part, channels))] * peers,
        scratch_shapes=[
            pltpu.VMEM((rows, channels), jnp.bfloat16),
            pltpu.VMEM((3, rows, channels), jnp.bfloat16),
            pltpu.VMEM((rows, channels), jnp.bfloat16),
        ],
        compiler_params=grant(20),
        name="backward",
    )(me_arg, order, conv_taps, *weights, *map(on_chip, (query, key, value, prob)), *map(on_chip, grad_blocks))
    received = [block.reshape(frame_rows, toks, channels) for block in spread_frames(results)]
    late = far_first(peers)[-3:-1]
    early = [mask for mask in range(peers) if mask not in late]
    output = None
    for masks in (early, late):
        blocks = [on_chip(received[mask]) for mask in masks]
        output = pl.pallas_call(
            functools.partial(place_kernel, masks=masks),
            in_specs=[smem] + [vmem] * len(masks) + [hbm] * (output is not None),
            out_specs=hbm,
            out_shape=jax.ShapeDtypeStruct(split, jnp.bfloat16),
            scratch_shapes=[pltpu.SemaphoreType.DMA((len(masks),))],
            input_output_aliases={} if output is None else {len(masks) + 1: 0},
            compiler_params=grant(4),
            name="place",
        )(me_arg, *blocks, *([] if output is None else [output]))
    return output.reshape(frame_rows, tile_rows, channels)


def solution(mesh):
    in_specs = (P("orbit", "tile", None), P("orbit", "tile", None), P(), P(), P(), P(), P())
    out_specs = P("orbit", "tile", None)
    return jax.shard_map(body, mesh=mesh, in_specs=in_specs, out_specs=out_specs, check_vma=False)
```
